32 devices in a mesh: groups: 2 (over y), blk: 4 (over z), rep: 2 (over x), sub: 2 (over core).
Axes of the slice: x: 2, y: 2, z: 4, core: 2. Of those that a mesh axis runs over, the one named last changes fastest.
Arguments:
- positions: float32 [3, 12288], P(None, ('groups', 'blk', 'rep', 'sub')), parts along dimension 1, may hold values from -19 to 19
- velocities: float32 [3, 12288], P(None, ('groups', 'blk', 'rep', 'sub')), parts along dimension 1, may hold values from -6 to 6
- charges: float32 [12288], P(('groups', 'blk', 'rep', 'sub')), parts along dimension 0, may hold values from -2.4 to 2.4
- dipoles: float32 [3, 12288], P(None, ('groups', 'blk', 'rep', 'sub')), parts along dimension 1, may hold values from -1.8 to 1.8
- quadrupoles: float32 [6, 12288], P(None, ('groups', 'blk', 'rep', 'sub')), parts along dimension 1, may hold values from -1.2 to 1.2
- damping: float32 [12288], P(('groups', 'blk', 'rep', 'sub')), parts along dimension 0, may hold values from 0.5 to 2
- inverse_mass: float32 [12288], P(('groups', 'blk', 'rep', 'sub')), parts along dimension 0, may hold values from 0.0625 to 1
- bonds: int32 [2, 12288], P(None, ('groups', 'blk', 'rep', 'sub')), parts along dimension 1, may hold values from 0 to 767
- bond_length: float32 [12288], P(('groups', 'blk', 'rep', 'sub')), parts along dimension 0, may hold values from 1 to 4
- angles: int32 [3, 24576], P(None, ('groups', 'blk', 'rep', 'sub')), parts along dimension 1, may hold values from 0 to 767
- torsions: int32 [4, 24576], P(None, ('groups', 'blk', 'rep', 'sub')), parts along dimension 1, may hold values from 0 to 767
Outputs:
- new_positions: float32 [3, 12288], P(None, ('groups', 'blk', 'rep', 'sub')), parts along dimension 1
- new_velocities: float32 [3, 12288], P(None, ('groups', 'blk', 'rep', 'sub')), parts along dimension 1
- slow_force: float32 [3, 12288], P(None, ('groups', 'blk', 'rep', 'sub')), parts along dimension 1
- slow_torque: float32 [3, 12288], P(None, ('groups', 'blk', 'rep', 'sub')), parts along dimension 1
The draws below stay inside these ranges and needn't reach their ends.
There are 2 independent parts, one for each index of `groups`. The reference program is written for one: setup_inputs(seed, part) draws one part's arguments, and reference() takes and returns one part's arrays. A program takes and returns all parts, laid end to end along the dimension named above; each array names one. Nothing has to cross between parts.
Inputs may be any that keep to these rules, and one draw needn't show every extreme that they name: `bonds`: bond term k indexes atoms of domain k // 768, counted within it. `angles`: angle term k indexes atoms of domain k // 1536, counted within it. `torsions`: torsion term k indexes atoms of domain k // 1536, counted within it.
All inputs are finite; a program needn't handle non-finite values.
Results may differ from the reference program's by a relative error of at most 0.0003.
Values sent between devices are 32-bit elements; how exact they have to be, the bound alone decides.
A program may use at most 64 MiB of HBM per device.

```python
import math
import jax
import jax.numpy as jnp
from jax import lax

ATOM_DEV = 384
INNER = 4
ATOMS = 6144
DOMAIN_ATOMS = 768
BONDS = 6144
ANGLES = 12288
TORSIONS = 12288


def draw_positions(key, part):
    key_centre = jax.random.fold_in(key, 11)
    key_offset = jax.random.fold_in(key, 12)
    centres = jax.random.uniform(key_centre, (3, ATOMS // DOMAIN_ATOMS), jnp.float32, -10.0, 10.0)
    offsets = jnp.clip(3.0 * jax.random.normal(key_offset, (3, ATOMS), jnp.float32), -9.0, 9.0)
    return jnp.repeat(centres, DOMAIN_ATOMS, axis=1) + offsets


def with_ends(drawn, rng, smallest, top_value):
    longest = drawn.shape.index(max(drawn.shape))
    spots = []
    for shift in (0, 1):
        where = [jax.random.randint(jax.random.fold_in(rng, axis), (), 0, length) for axis, length in enumerate(drawn.shape)]
        where[longest] = (where[longest] + shift) % drawn.shape[longest]
        spots.append(tuple(where))
    return drawn.at[spots[0]].set(smallest).at[spots[1]].set(top_value)


def level_of(rng, shape, pieces, low, high):
    def one(axis_at, blocks):
        draws = jax.random.uniform(jax.random.fold_in(jax.random.fold_in(rng, 6), axis_at), (blocks,), jnp.float32, low / len(pieces), high / len(pieces))
        return jnp.repeat(jnp.exp(draws), shape[axis_at] // blocks).reshape((-1,) + (1,) * (len(shape) - axis_at - 1))

    loudness = one(*pieces[0])
    for cut in pieces[1:]:
        loudness = loudness * one(*cut)
    return loudness


def noise(own_key, shape, deviation, reach, cuts=(), kind=jnp.bfloat16):
    entries = jax.random.normal(own_key, shape, jnp.float32) * deviation
    if len(cuts) > 0:
        entries = level_of(own_key, shape, cuts, -0.22, 0.18) * entries
    return jnp.clip(entries, min=-reach, max=reach).astype(kind)


def setup_inputs(seed: int = 0, part: int = 0) -> dict:
    streams_of = jax.random.split(jax.random.key(seed), 12)
    part_keys = jax.random.split(jax.random.fold_in(streams_of[11], part), 12)
    positions = draw_positions(jax.random.fold_in(jax.random.fold_in(streams_of[11], part), 71), part)
    velocities = noise(part_keys[1], (3, ATOMS), 1.0, 6.0, ((1, 16),), jnp.float32)
    charges = noise(part_keys[2], (ATOMS,), 0.4, 2.4, ((0, 16),), jnp.float32)
    dipoles = noise(part_keys[3], (3, ATOMS), 0.3, 1.8, ((1, 16),), jnp.float32)
    quadrupoles = noise(part_keys[4], (6, ATOMS), 0.2, 1.2, ((1, 16),), jnp.float32)
    damping = jnp.clip(jnp.exp(math.log(2.0) - 1.3862944 * jax.random.uniform(part_keys[5], (ATOMS,), jnp.float32) ** level_of(part_keys[5], (ATOMS,), ((0, 16),), -0.2, 0.2)), 0.5, 2.0)
    inverse_mass = jnp.clip(jnp.exp(math.log(1.0) - 2.7725887 * jax.random.uniform(part_keys[6], (ATOMS,), jnp.float32) ** level_of(part_keys[6], (ATOMS,), ((0, 16),), -0.2, 0.2)), 0.0625, 1.0)
    bonds = with_ends(jax.random.randint(part_keys[7], (2, BONDS), 0, DOMAIN_ATOMS), jax.random.fold_in(part_keys[7], 1), 0, DOMAIN_ATOMS - 1).astype(jnp.int32)
    bond_length = jnp.clip(1.0 + 3.0 * jax.random.uniform(part_keys[8], (BONDS,), jnp.float32) ** level_of(part_keys[8], (BONDS,), ((0, 16),), -0.2, 0.2), 1.0, 4.0)
    angles = with_ends(jax.random.randint(part_keys[9], (3, ANGLES), 0, DOMAIN_ATOMS), jax.random.fold_in(part_keys[9], 1), 0, DOMAIN_ATOMS - 1).astype(jnp.int32)
    torsions = with_ends(jax.random.randint(part_keys[10], (4, TORSIONS), 0, DOMAIN_ATOMS), jax.random.fold_in(part_keys[10], 1), 0, DOMAIN_ATOMS - 1).astype(jnp.int32)
    return dict(positions=positions, velocities=velocities, charges=charges, dipoles=dipoles, quadrupoles=quadrupoles, damping=damping, inverse_mass=inverse_mass, bonds=bonds, bond_length=bond_length, angles=angles, torsions=torsions)


QUAD_INDEX = ((0, 1, 2), (1, 3, 4), (2, 4, 5))
BOND_K = 0.3
ANGLE_K = 4.0
ANGLE_REST = -0.33
TORSION_K = 2.0
OUTER_DT = 0.2

def inner3(left, right):
    return left[0] * right[0] + left[1] * right[1] + left[2] * right[2]

def pair_energy(target_pos, target_dip, target_quad, target_charge, target_damp, source, target_ids, source_ids):
    separation = [source[c][None, :] - target_pos[c][:, None] for c in range(3)]
    dist_sq = inner3(separation, separation) + target_damp[:, None] * source[13][None, :]
    inv_one = lax.rsqrt(dist_sq)
    inv_three = inv_one / dist_sq
    inv_five = 3.0 * inv_three / dist_sq
    inv_seven = 5.0 * inv_five / dist_sq
    inv_nine = 7.0 * inv_seven / dist_sq
    charge_i = target_charge[:, None]
    charge_k = source[3][None, :]
    dip_i = [target_dip[c][:, None] for c in range(3)]
    dip_k = [source[4 + c][None, :] for c in range(3)]
    quad_i = [[target_quad[QUAD_INDEX[a][b]][:, None] for b in range(3)] for a in range(3)]
    quad_k = [[source[7 + QUAD_INDEX[a][b]][None, :] for b in range(3)] for a in range(3)]
    quad_ir = [inner3(quad_i[a], separation) for a in range(3)]
    quad_kr = [inner3(quad_k[a], separation) for a in range(3)]
    dip_ir = inner3(dip_i, separation)
    dip_kr = inner3(dip_k, separation)
    dip_ik = inner3(dip_i, dip_k)
    quad_rri = inner3(quad_ir, separation)
    quad_rrk = inner3(quad_kr, separation)
    quad_rrik = inner3(quad_ir, quad_kr)
    quad_ik = sum((quad_i[a][b] * quad_k[a][b] for a in range(3) for b in range(3)))
    dip_iqk = inner3(dip_i, quad_kr)
    dip_kqi = inner3(dip_k, quad_ir)
    term_one = charge_i * charge_k
    term_two = charge_k * dip_ir - charge_i * dip_kr + dip_ik
    term_three = charge_i * quad_rrk + charge_k * quad_rri - dip_ir * dip_kr + 2.0 * (dip_kqi - dip_iqk + quad_ik)
    term_four = dip_ir * quad_rrk - dip_kr * quad_rri - 4.0 * quad_rrik
    term_five = quad_rri * quad_rrk
    energy = term_one * inv_one + term_two * inv_three + term_three * inv_five + term_four * inv_seven + term_five * inv_nine
    distinct = target_ids[:, None] != source_ids[None, :]
    return jnp.sum(jnp.where(distinct, energy, 0.0))

def pair_gradients(target, source, target_ids, source_ids):

    def tile_energy(target_pos, target_dip, target_quad):
        return pair_energy(target_pos, target_dip, target_quad, target[3], target[13], source, target_ids, source_ids)
    grads = jax.grad(tile_energy, argnums=(0, 1, 2))(target[0:3], target[4:7], target[7:13])
    return jnp.concatenate(grads, 0)

def finish(partials, dipoles, quadrupoles):
    slow_force = -partials[0:3]
    field_dip = -partials[3:6]
    grad_quad = partials[6:12]
    halves = (1.0, 0.5, 0.5, 1.0, 0.5, 1.0)
    grad_matrix = [[halves[QUAD_INDEX[a][b]] * grad_quad[QUAD_INDEX[a][b]] for b in range(3)] for a in range(3)]
    quad_matrix = [[quadrupoles[QUAD_INDEX[a][b]] for b in range(3)] for a in range(3)]
    product = [[quad_matrix[a][0] * grad_matrix[0][b] + quad_matrix[a][1] * grad_matrix[1][b] + quad_matrix[a][2] * grad_matrix[2][b] for b in range(3)] for a in range(3)]
    torque = jnp.stack([dipoles[1] * field_dip[2] - dipoles[2] * field_dip[1] - 2.0 * (product[1][2] - product[2][1]), dipoles[2] * field_dip[0] - dipoles[0] * field_dip[2] - 2.0 * (product[2][0] - product[0][2]), dipoles[0] * field_dip[1] - dipoles[1] * field_dip[0] - 2.0 * (product[0][1] - product[1][0])])
    return (slow_force, torque)

def bonded_energy(coords, bonds, bond_length, angles, torsions):

    def picked(rows):
        return coords[:, rows]
    stretch = picked(bonds[1]) - picked(bonds[0])
    length_now = jnp.sqrt(lax.optimization_barrier(jnp.sum(stretch * stretch, 0)) + 0.01)
    bond_gap = length_now - bond_length
    bond_part = 0.5 * BOND_K * jnp.sum(bond_gap * bond_gap)
    arm_first = picked(angles[0]) - picked(angles[1])
    arm_second = picked(angles[2]) - picked(angles[1])
    cosine = lax.optimization_barrier(jnp.sum(arm_first * arm_second, 0)) * lax.rsqrt((lax.optimization_barrier(jnp.sum(arm_first * arm_first, 0)) + 0.01) * (lax.optimization_barrier(jnp.sum(arm_second * arm_second, 0)) + 0.01))
    angle_gap = cosine - ANGLE_REST
    angle_part = 0.5 * ANGLE_K * jnp.sum(angle_gap * angle_gap)
    bond_one = picked(torsions[1]) - picked(torsions[0])
    bond_two = picked(torsions[2]) - picked(torsions[1])
    bond_three = picked(torsions[3]) - picked(torsions[2])
    normal_one = jnp.cross(bond_one, bond_two, axis=0)
    normal_two = jnp.cross(bond_two, bond_three, axis=0)
    dihedral = lax.optimization_barrier(jnp.sum(normal_one * normal_two, 0)) * lax.rsqrt((lax.optimization_barrier(jnp.sum(normal_one * normal_one, 0)) + 0.1) * (lax.optimization_barrier(jnp.sum(normal_two * normal_two, 0)) + 0.1))
    torsion_part = TORSION_K * jnp.sum(1.0 + dihedral)
    return bond_part + angle_part + torsion_part

def reference(positions, velocities, charges, dipoles, quadrupoles, damping, inverse_mass, bonds, bond_length, angles, torsions):
    record = jnp.concatenate([positions, charges[None, :], dipoles, quadrupoles, damping[None, :]], 0)
    atom_ids = jnp.arange(ATOMS, dtype=jnp.int32)
    target_width = ATOM_DEV
    source_width = 2 * ATOM_DEV
    target_blocks = record.reshape(14, ATOMS // target_width, target_width).transpose(1, 0, 2)
    target_idblk = atom_ids.reshape(ATOMS // target_width, target_width)
    source_blocks = record.reshape(14, ATOMS // source_width, source_width).transpose(1, 0, 2)
    source_idblk = atom_ids.reshape(ATOMS // source_width, source_width)

    def one_target(packed):
        target, target_ids = packed

        def add_source(summed, source_pack):
            source, source_ids = source_pack
            return (summed + pair_gradients(target, source, target_ids, source_ids), None)
        summed, _unused = lax.scan(add_source, jnp.zeros((12, target_width), jnp.float32), (source_blocks, source_idblk))
        return summed
    partials = lax.map(one_target, (target_blocks, target_idblk)).transpose(1, 0, 2).reshape(12, ATOMS)
    slow_force, slow_torque = finish(partials, dipoles, quadrupoles)
    bond_offset = jnp.arange(ATOMS, dtype=jnp.int32) // DOMAIN_ATOMS * DOMAIN_ATOMS
    term_offset = jnp.arange(2 * ATOMS, dtype=jnp.int32) // (2 * DOMAIN_ATOMS) * DOMAIN_ATOMS
    global_bonds = bonds + bond_offset[None, :]
    global_angles = angles + term_offset[None, :]
    global_torsions = torsions + term_offset[None, :]

    def bonded_push(coords):
        return -jax.grad(bonded_energy)(coords, global_bonds, bond_length, global_angles, global_torsions)
    inner_dt = OUTER_DT / INNER
    velocity = velocities + 0.5 * OUTER_DT * slow_force * inverse_mass[None, :]
    coords = positions
    push = bonded_push(coords)
    for substep in range(INNER):
        velocity = velocity + 0.5 * inner_dt * push * inverse_mass[None, :]
        coords = coords + inner_dt * velocity
        push = bonded_push(coords)
        velocity = velocity + 0.5 * inner_dt * push * inverse_mass[None, :]
    return (coords, velocity, slow_force, slow_torque)
```

```python
import functools

import jax
import jax.numpy as jnp
from jax import lax
from jax.experimental import pallas as pl
from jax.experimental.pallas import tpu as pltpu
from jax.sharding import PartitionSpec as P

INNER = 4
MESH = pl.DeviceIdType.MESH
LANES = 128
QUAD_INDEX = ((0, 1, 2), (1, 3, 4), (2, 4, 5))
BOND_K = 0.3
ANGLE_K = 4.0
ANGLE_REST = -0.33
TORSION_K = 2.0
OUTER_DT = 0.2
UNROLL = 3


def dot3(left, right):
    return left[0] * right[0] + left[1] * right[1] + left[2] * right[2]


def matvec(quad, vec):
    return [dot3([quad[QUAD_INDEX[a][b]] for b in range(3)], vec) for a in range(3)]


def my_place():
    n_rep = lax.axis_size("rep")
    n_sub = lax.axis_size("sub")
    return (lax.axis_index("blk") * n_rep + lax.axis_index("rep")) * n_sub + lax.axis_index("sub")


def device_at(place):
    n_rep = lax.axis_size("rep")
    n_sub = lax.axis_size("sub")
    return (
        lax.axis_index("groups"),
        place // (n_rep * n_sub),
        (place // n_sub) % n_rep,
        place % n_sub,
    )


def greet(half, place, count):
    barrier = pltpu.get_barrier_semaphore()

    def one(j, _):
        for other in ((place + j) % count, (place + count - j) % count):
            pl.semaphore_signal(
                barrier, inc=1, device_id=device_at(other), device_id_type=MESH
            )
        return 0

    lax.fori_loop(1, half + 1, one, 0)
    pl.semaphore_wait(barrier, 2 * half)


def gather_kernel(count, own_ref, out_ref, send_sem, recv_sem):
    half = count // 2
    width = own_ref.shape[1]
    place = my_place()
    greet(half, place, count)

    def copy(j):
        return pltpu.make_async_remote_copy(
            src_ref=own_ref,
            dst_ref=out_ref.at[:, pl.ds(pl.multiple_of(j * width, LANES), width)],
            send_sem=send_sem.at[j],
            recv_sem=recv_sem.at[j],
            device_id=device_at((place + count - j) % count),
            device_id_type=MESH,
        )

    def start(j, _):
        copy(j).start()
        return 0

    def finish_one(j, _):
        copy(j).wait()
        return 0

    lax.fori_loop(1, half + 1, start, 0)
    out_ref[:, 0:width] = own_ref[...]
    lax.fori_loop(1, half + 1, finish_one, 0)


def reduce_kernel(count, part_ref, out_ref, land_ref, send_sem, recv_sem):
    half = count // 2
    width = out_ref.shape[1]
    place = my_place()
    greet(half, place, count)

    def copy(j):
        return pltpu.make_async_remote_copy(
            src_ref=part_ref.at[:, pl.ds(pl.multiple_of(j * width, LANES), width)],
            dst_ref=land_ref.at[j],
            send_sem=send_sem.at[j],
            recv_sem=recv_sem.at[j],
            device_id=device_at((place + j) % count),
            device_id_type=MESH,
        )

    def start(j, _):
        copy(j).start()
        return 0

    def finish_one(j, total):
        copy(j).wait()
        return total + land_ref[j]

    lax.fori_loop(1, half + 1, start, 0)
    out_ref[...] = lax.fori_loop(1, half + 1, finish_one, part_ref[:, 0:width])


def pair_terms(target, source, alive):
    c_i, d_i, q_i = target[3], target[4:7], target[7:13]
    c_k, d_k, q_k = source[3], source[4:7], source[7:13]
    r = [source[c] - target[c] for c in range(3)]
    s = dot3(r, r) + target[13] * source[13]
    root = lax.rsqrt(s)
    b1 = alive(root)
    inv = root * root
    b3 = b1 * inv
    b5 = b3 * (3.0 * inv)
    b7 = b5 * (5.0 * inv)
    b9 = b7 * (7.0 * inv)
    b11 = b9 * (9.0 * inv)
    f5 = 2.0 * b5
    f7 = 4.0 * b7
    f10 = 4.0 * b5
    w = matvec(q_k, r)
    u = matvec(q_i, r)
    dk = dot3(d_k, r)
    qk = dot3(w, r)
    di = dot3(d_i, r)
    qi = dot3(u, r)
    a_i = c_k * b3 - dk * b5 + qk * b7
    b_i = c_k * b5 - dk * b7 + qk * b9
    g_i = c_k * b7 - dk * b9 + qk * b11
    a_k = c_i * b3 + di * b5 + qi * b7
    b_k = c_i * b5 + di * b7 + qi * b9
    h_i = [f5 * d_k[a] - f7 * w[a] for a in range(3)]
    h_k = [f5 * d_i[a] + f7 * u[a] for a in range(3)]
    br_i = [b_i * r[a] for a in range(3)]
    br_k = [b_k * r[a] for a in range(3)]
    v_i = [br_i[a] + h_i[a] for a in range(3)]
    v_k = [br_k[a] - h_k[a] for a in range(3)]
    on_i = matvec(q_i, [v_i[a] + br_i[a] for a in range(3)])
    on_k = matvec(q_k, [v_k[a] + br_k[a] for a in range(3)])
    qm = (q_i[0] * q_k[0] + q_i[3] * q_k[3] + q_i[5] * q_k[5]) + 2.0 * (
        q_i[1] * q_k[1] + q_i[2] * q_k[2] + q_i[4] * q_k[4]
    )
    alpha = (
        c_i * a_i
        + di * b_i
        + qi * g_i
        + 0.5 * (dot3(d_i, h_i) + f7 * (dot3(d_k, u) + qm))
        - (4.0 * b9) * dot3(u, w)
    )
    push = [
        (a_i * d_i[a] - a_k * d_k[a]) + (on_i[a] + on_k[a]) - alpha * r[a] for a in range(3)
    ]

    def quad_rows(v, q):
        return [
            r[0] * v[0] + f5 * q[0],
            (r[0] * v[1] + r[1] * v[0]) + f10 * q[1],
            (r[0] * v[2] + r[2] * v[0]) + f10 * q[2],
            r[1] * v[1] + f5 * q[3],
            (r[1] * v[2] + r[2] * v[1]) + f10 * q[4],
            r[2] * v[2] + f5 * q[5],
        ]

    f_i = [a_i * r[a] + b3 * d_k[a] - f5 * w[a] for a in range(3)]
    f_k = [b3 * d_i[a] + f5 * u[a] - a_k * r[a] for a in range(3)]
    return push, f_i + quad_rows(v_i, q_k), f_k + quad_rows(v_k, q_i)


def pair_kernel(count, own_ref, all_ref, out_ref, acc_ref, tgt_ref):
    half = count // 2
    rows = own_ref.shape[0]
    chunks = rows // LANES
    lower = my_place() < half
    lane = lax.broadcasted_iota(jnp.int32, (8, LANES), 1)
    sublane = lax.broadcasted_iota(jnp.int32, (8, LANES), 0)
    diff = lane - sublane
    acc_ref[...] = jnp.zeros_like(acc_ref)
    zero = jnp.zeros((8, LANES), jnp.float32)

    def source_at(start):
        return [all_ref[c : c + 1, pl.ds(start, LANES)] for c in range(14)]

    def one_group(group, _):
        base = pl.multiple_of(group * 8, 8)
        target = [
            jnp.broadcast_to(own_ref[pl.ds(base, 8), c : c + 1], (8, LANES)) for c in range(14)
        ]

        def near(chunk, sums):
            start = pl.multiple_of(chunk * LANES, LANES)

            def alive(root):
                return jnp.where(diff == base - start, 0.0, root)

            push, on_i, _ = pair_terms(target, source_at(start), alive)
            return tuple(x + y for x, y in zip(sums, push + on_i))

        def far(chunk, sums):
            start = pl.multiple_of(chunk * LANES, LANES)
            push, on_i, on_k = pair_terms(target, source_at(start), lambda root: root)
            for c in range(3):
                acc_ref[8 * c : 8 * c + 8, pl.ds(start, LANES)] -= push[c]
            for c in range(9):
                acc_ref[24 + 8 * c : 32 + 8 * c, pl.ds(start, LANES)] += on_k[c]
            return tuple(x + y for x, y in zip(sums, push + on_i))

        first = lax.rem(base // LANES + jnp.where(lower, 0, 1), 2)

        def last(step, sums):
            return far(half * chunks + first + 2 * step, sums)

        sums = lax.fori_loop(0, chunks, near, (zero,) * 12)
        sums = lax.fori_loop(chunks, half * chunks, far, sums, unroll=UNROLL)
        sums = lax.fori_loop(0, (chunks - first + 1) // 2, last, sums)
        tgt_ref[pl.ds(base, 8), :] = jnp.concatenate(
            [jnp.sum(x, axis=1, keepdims=True) for x in sums]
            + [jnp.zeros((8, LANES - 12), jnp.float32)],
            axis=1,
        )
        return 0

    lax.fori_loop(0, rows // 8, one_group, 0)

    def fold(chunk, _):
        at = pl.ds(pl.multiple_of(chunk * LANES, LANES), LANES)
        out_ref[:, at] = jnp.concatenate(
            [jnp.sum(acc_ref[8 * c : 8 * c + 8, at], axis=0, keepdims=True) for c in range(12)]
            + [jnp.zeros((4, LANES), jnp.float32)],
            axis=0,
        )
        return 0

    lax.fori_loop(chunks, (half + 1) * chunks, fold, 0)
    for c in range(chunks):
        flipped = tgt_ref[c * LANES : (c + 1) * LANES, :].T
        out_ref[:, c * LANES : (c + 1) * LANES] = flipped[0:16]


def finish(sums, dipoles, quadrupoles):
    q = [quadrupoles[c] for c in range(6)]
    d = [dipoles[c] for c in range(3)]
    force = sums[0:3]
    field = [-sums[3 + a] for a in range(3)]
    halves = (1.0, 0.5, 0.5, 1.0, 0.5, 1.0)
    g = [halves[c] * sums[6 + c] for c in range(6)]

    def product(a, b):
        return dot3(
            [q[QUAD_INDEX[a][c]] for c in range(3)], [g[QUAD_INDEX[c][b]] for c in range(3)]
        )

    torque = jnp.stack(
        [
            d[1] * field[2] - d[2] * field[1] - 2.0 * (product(1, 2) - product(2, 1)),
            d[2] * field[0] - d[0] * field[2] - 2.0 * (product(2, 0) - product(0, 2)),
            d[0] * field[1] - d[1] * field[0] - 2.0 * (product(0, 1) - product(1, 0)),
        ]
    )
    return force, torque


def cross3(a, b):
    return [
        a[1] * b[2] - a[2] * b[1],
        a[2] * b[0] - a[0] * b[2],
        a[0] * b[1] - a[1] * b[0],
    ]


def minus(a, b):
    return [x - y for x, y in zip(a, b)]


def bond_push(first, second, rest):
    step = minus(second, first)
    sq = dot3(step, step) + 0.01
    scale = BOND_K * (1.0 - rest * lax.rsqrt(sq))
    pull = [scale * x for x in step]
    return [pull, [-x for x in pull]]


def angle_push(first, centre, third):
    a = minus(first, centre)
    b = minus(third, centre)
    ia = lax.rsqrt(dot3(a, a) + 0.01)
    ib = lax.rsqrt(dot3(b, b) + 0.01)
    cosine = dot3(a, b) * (ia * ib)
    lead = -ANGLE_K * (cosine - ANGLE_REST)
    both = lead * (ia * ib)
    on_a = lead * cosine * (ia * ia)
    on_b = lead * cosine * (ib * ib)
    fa = [both * y - on_a * x for x, y in zip(a, b)]
    fb = [both * x - on_b * y for x, y in zip(a, b)]
    return [fa, [-x - y for x, y in zip(fa, fb)], fb]


def torsion_push(p0, p1, p2, p3):
    one = minus(p1, p0)
    two = minus(p2, p1)
    three = minus(p3, p2)
    m = cross3(one, two)
    n = cross3(two, three)
    im = lax.rsqrt(dot3(m, m) + 0.1)
    in_ = lax.rsqrt(dot3(n, n) + 0.1)
    both = -TORSION_K * (im * in_)
    dih = dot3(m, n) * both
    cm = dih * (im * im)
    cn = dih * (in_ * in_)
    gm = [both * y - cm * x for x, y in zip(m, n)]
    gn = [both * x - cn * y for x, y in zip(m, n)]
    f_one = cross3(two, gm)
    f_three = cross3(gn, two)
    f_two = [x + y for x, y in zip(cross3(gm, one), cross3(three, gn))]
    return [
        [-x for x in f_one],
        minus(f_one, f_two),
        minus(f_two, f_three),
        f_three,
    ]


def split3(x):
    top = x.astype(jnp.bfloat16)
    rest = x - top.astype(jnp.float32)
    mid = rest.astype(jnp.bfloat16)
    low = (rest - mid.astype(jnp.float32)).astype(jnp.bfloat16)
    return jnp.concatenate([top, mid, low], axis=0)


def merge3(x):
    n = x.shape[0] // 3
    return x[0:n] + x[n : 2 * n] + x[2 * n : 3 * n]


def bonded_kernel(high, n_bond, n_term, pos_ref, vel_ref, slow_ref, mass_ref, idx_ref, len_ref, x_out, v_out, lo_ref, hi_ref):
    total = idx_ref.shape[1]
    index = idx_ref[...]
    hi_part = index // LANES
    lo_part = index - hi_part * LANES
    lo_rows = lax.broadcasted_iota(jnp.int32, (LANES, total), 0)
    lo_ref[...] = jnp.where(lo_rows == lo_part, 1.0, 0.0).astype(jnp.bfloat16)
    hi_rows = lax.broadcasted_iota(jnp.int32, (high, total), 0)
    hi_ref[...] = jnp.where(hi_rows == hi_part, 1.0, 0.0)
    mass = jnp.concatenate([mass_ref[...]] * 3, axis=0)
    rest = len_ref[...]

    def push_at(coords):
        looked = merge3(
            jnp.dot(split3(coords), lo_ref[...], preferred_element_type=jnp.float32)
        )
        hi = hi_ref[...]
        row = [
            jnp.sum(looked[c * high : (c + 1) * high] * hi, axis=0, keepdims=True)
            for c in range(3)
        ]
        cuts = [(0, n_bond), (n_bond, 2 * n_bond)]
        cuts += [(2 * n_bond + j * n_term, 2 * n_bond + (j + 1) * n_term) for j in range(7)]
        atoms = [[row[c][:, lo:up] for c in range(3)] for lo, up in cuts]
        pushes = (
            bond_push(atoms[0], atoms[1], rest)
            + angle_push(*atoms[2:5])
            + torsion_push(*atoms[5:9])
        )
        spread = jnp.concatenate(
            [jnp.concatenate([p[c] for p in pushes], axis=1) * hi for c in range(3)], axis=0
        )
        return merge3(
            lax.dot_general(
                split3(spread),
                lo_ref[...],
                (((1,), (1,)), ((), ())),
                preferred_element_type=jnp.float32,
            )
        )

    dt = OUTER_DT / INNER
    x = pos_ref[...]
    v = vel_ref[...] + (0.5 * OUTER_DT) * slow_ref[...] * mass
    half = (0.5 * dt) * mass
    v = v + half * push_at(x)

    def substep(step, carry):
        x, v = carry
        x = x + dt * v
        kick = half * push_at(x)
        v = v + kick
        v = v + jnp.where(step < INNER - 1, kick, 0.0)
        return x, v

    x, v = lax.fori_loop(0, INNER, substep, (x, v))
    x_out[...] = x
    v_out[...] = v


def body(
    positions,
    velocities,
    charges,
    dipoles,
    quadrupoles,
    damping,
    inverse_mass,
    bonds,
    bond_length,
    angles,
    torsions,
):
    atoms = positions.shape[1]
    n_sub = lax.axis_size("sub")
    sub = lax.axis_index("sub")
    record = jnp.concatenate(
        [positions, charges[None, :], dipoles, quadrupoles, damping[None, :]], 0
    )
    padded = jnp.concatenate([record, jnp.zeros((2, atoms), jnp.float32)], 0)
    own = padded.T
    count = lax.axis_size("blk") * lax.axis_size("rep") * n_sub
    half = count // 2
    slots = half + 1
    vmem = pl.BlockSpec(memory_space=pltpu.VMEM)

    def remote(kernel, name, ident, width, scratch):
        return pl.pallas_call(
            functools.partial(kernel, count),
            out_shape=jax.ShapeDtypeStruct((16, width), jnp.float32),
            in_specs=[vmem],
            out_specs=vmem,
            scratch_shapes=scratch
            + [pltpu.SemaphoreType.DMA((slots,)), pltpu.SemaphoreType.DMA((slots,))],
            compiler_params=pltpu.CompilerParams(
                collective_id=ident, vmem_limit_bytes=48 * 1024 * 1024
            ),
            name=name,
        )

    everyone = remote(gather_kernel, "gather", 1, slots * atoms, [])(padded)
    parts = pl.pallas_call(
        functools.partial(pair_kernel, count),
        out_shape=jax.ShapeDtypeStruct((16, slots * atoms), jnp.float32),
        in_specs=[vmem, vmem],
        out_specs=vmem,
        scratch_shapes=[
            pltpu.VMEM((96, slots * atoms), jnp.float32),
            pltpu.VMEM((atoms, LANES), jnp.float32),
        ],
        compiler_params=pltpu.CompilerParams(vmem_limit_bytes=48 * 1024 * 1024),
        name="pairs",
    )(own, everyone)
    sums = remote(
        reduce_kernel, "reduce", 2, atoms, [pltpu.VMEM((slots, 16, atoms), jnp.float32)]
    )(parts)
    slow_force, slow_torque = finish(sums, dipoles, quadrupoles)

    def both(mine):
        return lax.all_gather(mine, "sub", axis=1, tiled=True)

    n_term = angles.shape[1] * n_sub
    n_bond = bonds.shape[1] * n_sub
    shared = both(
        jnp.concatenate(
            [positions, velocities, inverse_mass[None, :], bond_length[None, :]], 0
        )
    )
    bonds_all = both(bonds)
    terms_all = both(jnp.concatenate([angles, torsions], 0))
    index = jnp.concatenate([bonds_all.reshape(-1), terms_all.reshape(-1)])[None, :]
    slow_all = both(slow_force)
    size = atoms * n_sub
    used = size // LANES
    high = -(-used // 8) * 8

    def tiled(rows):
        count = rows.shape[0]
        cut = rows.reshape(count, used, LANES)
        return jnp.pad(cut, ((0, 0), (0, high - used), (0, 0))).reshape(count * high, LANES)

    total = index.shape[1]

    def kernel(*refs):
        bonded_kernel(high, n_bond, n_term, *refs)

    state = jax.ShapeDtypeStruct((3 * high, LANES), jnp.float32)
    x_new, v_new = pl.pallas_call(
        kernel,
        out_shape=(state, state),
        in_specs=[vmem] * 6,
        out_specs=(vmem, vmem),
        scratch_shapes=[
            pltpu.VMEM((LANES, total), jnp.bfloat16),
            pltpu.VMEM((high, total), jnp.float32),
        ],
        compiler_params=pltpu.CompilerParams(vmem_limit_bytes=48 * 1024 * 1024),
        name="bonded",
    )(
        tiled(shared[0:3]),
        tiled(shared[3:6]),
        tiled(slow_all),
        tiled(shared[6:7]),
        index,
        shared[7:8],
    )

    def mine(state):
        flat = state.reshape(3, high * LANES)
        return lax.dynamic_slice_in_dim(flat, sub * atoms, atoms, axis=1)

    return (mine(x_new), mine(v_new), slow_force, slow_torque)


def solution(mesh):
    placed = (
        P(None, ("groups", "blk", "rep", "sub")),
        P(None, ("groups", "blk", "rep", "sub")),
        P(("groups", "blk", "rep", "sub")),
        P(None, ("groups", "blk", "rep", "sub")),
        P(None, ("groups", "blk", "rep", "sub")),
        P(("groups", "blk", "rep", "sub")),
        P(("groups", "blk", "rep", "sub")),
        P(None, ("groups", "blk", "rep", "sub")),
        P(("groups", "blk", "rep", "sub")),
        P(None, ("groups", "blk", "rep", "sub")),
        P(None, ("groups", "blk", "rep", "sub")),
    )
    return jax.shard_map(
        body,
        mesh=mesh,
        in_specs=placed,
        out_specs=(
            P(None, ("groups", "blk", "rep", "sub")),
            P(None, ("groups", "blk", "rep", "sub")),
            P(None, ("groups", "blk", "rep", "sub")),
            P(None, ("groups", "blk", "rep", "sub")),
        ),
        check_vma=False,
    )
```

```python
import functools

import jax
import jax.numpy as jnp
from jax import lax
from jax.experimental import pallas as pl
from jax.experimental.pallas import tpu as pltpu
from jax.sharding import PartitionSpec as P

INNER = 4
MESH = pl.DeviceIdType.MESH
LANES = 128
QUAD_INDEX = ((0, 1, 2), (1, 3, 4), (2, 4, 5))
BOND_K = 0.3
ANGLE_K = 4.0
ANGLE_REST = -0.33
TORSION_K = 2.0
OUTER_DT = 0.2
UNROLL = 3


def dot3(left, right):
    return left[0] * right[0] + left[1] * right[1] + left[2] * right[2]


def matvec(quad, vec):
    return [dot3([quad[QUAD_INDEX[a][b]] for b in range(3)], vec) for a in range(3)]


def my_place():
    n_rep = lax.axis_size("rep")
    n_sub = lax.axis_size("sub")
    return (lax.axis_index("blk") * n_rep + lax.axis_index("rep")) * n_sub + lax.axis_index("sub")


def device_at(place):
    n_rep = lax.axis_size("rep")
    n_sub = lax.axis_size("sub")
    return (
        lax.axis_index("groups"),
        place // (n_rep * n_sub),
        (place // n_sub) % n_rep,
        place % n_sub,
    )


def greet(half, place, count):
    barrier = pltpu.get_barrier_semaphore()

    def one(j, _):
        for other in ((place + j) % count, (place + count - j) % count):
            pl.semaphore_signal(
                barrier, inc=1, device_id=device_at(other), device_id_type=MESH
            )
        return 0

    lax.fori_loop(1, half + 1, one, 0)
    pl.semaphore_wait(barrier, 2 * half)


def gather_kernel(
    count, own_ref, pack_ref, out_ref, both_ref, send_sem, recv_sem, pack_send, pack_recv
):
    half = count // 2
    width = own_ref.shape[1]
    place = my_place()
    sub = lax.axis_index("sub")
    greet(half, place, count)

    def copy(j):
        return pltpu.make_async_remote_copy(
            src_ref=own_ref,
            dst_ref=out_ref.at[:, pl.ds(pl.multiple_of(j * width, LANES), width)],
            send_sem=send_sem.at[j],
            recv_sem=recv_sem.at[j],
            device_id=device_at((place + count - j) % count),
            device_id_type=MESH,
        )

    def start(j, _):
        copy(j).start()
        return 0

    def finish_one(j, _):
        copy(j).wait()
        return 0

    lax.fori_loop(1, half + 1, start, 0)
    swap = pltpu.make_async_remote_copy(
        src_ref=pack_ref,
        dst_ref=both_ref.at[sub],
        send_sem=pack_send,
        recv_sem=pack_recv,
        device_id=device_at(place + 1 - 2 * sub),
        device_id_type=MESH,
    )
    swap.start()
    out_ref[:, 0:width] = own_ref[...]
    both_ref[sub] = pack_ref[...]
    swap.wait()
    lax.fori_loop(1, half + 1, finish_one, 0)


def pair_terms(target, source, alive):
    c_i, d_i, q_i = target[3], target[4:7], target[7:13]
    c_k, d_k, q_k = source[3], source[4:7], source[7:13]
    r = [source[c] - target[c] for c in range(3)]
    s = dot3(r, r) + target[13] * source[13]
    root = lax.rsqrt(s)
    b1 = alive(root)
    inv = root * root
    b3 = b1 * inv
    b5 = b3 * (3.0 * inv)
    b7 = b5 * (5.0 * inv)
    b9 = b7 * (7.0 * inv)
    b11 = b9 * (9.0 * inv)
    f5 = 2.0 * b5
    f7 = 4.0 * b7
    f10 = 4.0 * b5
    w = matvec(q_k, r)
    u = matvec(q_i, r)
    dk = dot3(d_k, r)
    qk = dot3(w, r)
    di = dot3(d_i, r)
    qi = dot3(u, r)
    a_i = c_k * b3 - dk * b5 + qk * b7
    b_i = c_k * b5 - dk * b7 + qk * b9
    g_i = c_k * b7 - dk * b9 + qk * b11
    a_k = c_i * b3 + di * b5 + qi * b7
    b_k = c_i * b5 + di * b7 + qi * b9
    h_i = [f5 * d_k[a] - f7 * w[a] for a in range(3)]
    h_k = [f5 * d_i[a] + f7 * u[a] for a in range(3)]
    br_i = [b_i * r[a] for a in range(3)]
    br_k = [b_k * r[a] for a in range(3)]
    v_i = [br_i[a] + h_i[a] for a in range(3)]
    v_k = [br_k[a] - h_k[a] for a in range(3)]
    on_i = matvec(q_i, [v_i[a] + br_i[a] for a in range(3)])
    on_k = matvec(q_k, [v_k[a] + br_k[a] for a in range(3)])
    qm = (q_i[0] * q_k[0] + q_i[3] * q_k[3] + q_i[5] * q_k[5]) + 2.0 * (
        q_i[1] * q_k[1] + q_i[2] * q_k[2] + q_i[4] * q_k[4]
    )
    alpha = (
        c_i * a_i
        + di * b_i
        + qi * g_i
        + 0.5 * (dot3(d_i, h_i) + f7 * (dot3(d_k, u) + qm))
        - (4.0 * b9) * dot3(u, w)
    )
    push = [
        (a_i * d_i[a] - a_k * d_k[a]) + (on_i[a] + on_k[a]) - alpha * r[a] for a in range(3)
    ]

    def quad_rows(v, q):
        return [
            r[0] * v[0] + f5 * q[0],
            (r[0] * v[1] + r[1] * v[0]) + f10 * q[1],
            (r[0] * v[2] + r[2] * v[0]) + f10 * q[2],
            r[1] * v[1] + f5 * q[3],
            (r[1] * v[2] + r[2] * v[1]) + f10 * q[4],
            r[2] * v[2] + f5 * q[5],
        ]

    f_i = [a_i * r[a] + b3 * d_k[a] - f5 * w[a] for a in range(3)]
    f_k = [b3 * d_i[a] + f5 * u[a] - a_k * r[a] for a in range(3)]
    return push, f_i + quad_rows(v_i, q_k), f_k + quad_rows(v_k, q_i)


def pair_kernel(count, own_ref, all_ref, out_ref, acc_ref, tgt_ref):
    half = count // 2
    rows = own_ref.shape[0]
    chunks = rows // LANES
    lower = my_place() < half
    lane = lax.broadcasted_iota(jnp.int32, (8, LANES), 1)
    sublane = lax.broadcasted_iota(jnp.int32, (8, LANES), 0)
    diff = lane - sublane
    acc_ref[...] = jnp.zeros_like(acc_ref)
    zero = jnp.zeros((8, LANES), jnp.float32)

    def source_at(start):
        return [all_ref[c : c + 1, pl.ds(start, LANES)] for c in range(14)]

    def one_group(group, _):
        base = pl.multiple_of(group * 8, 8)
        target = [
            jnp.broadcast_to(own_ref[pl.ds(base, 8), c : c + 1], (8, LANES)) for c in range(14)
        ]

        def near(chunk, sums):
            start = pl.multiple_of(chunk * LANES, LANES)

            def alive(root):
                return jnp.where(diff == base - start, 0.0, root)

            push, on_i, _ = pair_terms(target, source_at(start), alive)
            return tuple(x + y for x, y in zip(sums, push + on_i))

        def far(chunk, sums):
            start = pl.multiple_of(chunk * LANES, LANES)
            push, on_i, on_k = pair_terms(target, source_at(start), lambda root: root)
            for c in range(3):
                acc_ref[8 * c : 8 * c + 8, pl.ds(start, LANES)] -= push[c]
            for c in range(9):
                acc_ref[24 + 8 * c : 32 + 8 * c, pl.ds(start, LANES)] += on_k[c]
            return tuple(x + y for x, y in zip(sums, push + on_i))

        first = lax.rem(base // LANES + jnp.where(lower, 0, 1), 2)

        def last(step, sums):
            return far(half * chunks + first + 2 * step, sums)

        sums = lax.fori_loop(0, chunks, near, (zero,) * 12)
        sums = lax.fori_loop(chunks, half * chunks, far, sums, unroll=UNROLL)
        sums = lax.fori_loop(0, (chunks - first + 1) // 2, last, sums)
        tgt_ref[pl.ds(base, 8), :] = jnp.concatenate(
            [jnp.sum(x, axis=1, keepdims=True) for x in sums]
            + [jnp.zeros((8, LANES - 12), jnp.float32)],
            axis=1,
        )
        return 0

    lax.fori_loop(0, rows // 8, one_group, 0)

    def fold(chunk, _):
        at = pl.ds(pl.multiple_of(chunk * LANES, LANES), LANES)
        out_ref[:, at] = jnp.concatenate(
            [jnp.sum(acc_ref[8 * c : 8 * c + 8, at], axis=0, keepdims=True) for c in range(12)]
            + [jnp.zeros((4, LANES), jnp.float32)],
            axis=0,
        )
        return 0

    lax.fori_loop(chunks, (half + 1) * chunks, fold, 0)
    for c in range(chunks):
        flipped = tgt_ref[c * LANES : (c + 1) * LANES, :].T
        out_ref[:, c * LANES : (c + 1) * LANES] = flipped[0:16]


def torque_of(sums, d, q):
    field = [-sums[3 + a] for a in range(3)]
    halves = (1.0, 0.5, 0.5, 1.0, 0.5, 1.0)
    g = [halves[c] * sums[6 + c] for c in range(6)]

    def product(a, b):
        return dot3(
            [q[QUAD_INDEX[a][c]] for c in range(3)], [g[QUAD_INDEX[c][b]] for c in range(3)]
        )

    return jnp.concatenate(
        [
            d[1] * field[2] - d[2] * field[1] - 2.0 * (product(1, 2) - product(2, 1)),
            d[2] * field[0] - d[0] * field[2] - 2.0 * (product(2, 0) - product(0, 2)),
            d[0] * field[1] - d[1] * field[0] - 2.0 * (product(0, 1) - product(1, 0)),
        ],
        axis=0,
    )


def cross3(a, b):
    return [
        a[1] * b[2] - a[2] * b[1],
        a[2] * b[0] - a[0] * b[2],
        a[0] * b[1] - a[1] * b[0],
    ]


def minus(a, b):
    return [x - y for x, y in zip(a, b)]


def bond_push(first, second, rest):
    step = minus(second, first)
    sq = dot3(step, step) + 0.01
    scale = BOND_K * (1.0 - rest * lax.rsqrt(sq))
    pull = [scale * x for x in step]
    return [pull, [-x for x in pull]]


def angle_push(first, centre, third):
    a = minus(first, centre)
    b = minus(third, centre)
    ia = lax.rsqrt(dot3(a, a) + 0.01)
    ib = lax.rsqrt(dot3(b, b) + 0.01)
    cosine = dot3(a, b) * (ia * ib)
    lead = -ANGLE_K * (cosine - ANGLE_REST)
    both = lead * (ia * ib)
    on_a = lead * cosine * (ia * ia)
    on_b = lead * cosine * (ib * ib)
    fa = [both * y - on_a * x for x, y in zip(a, b)]
    fb = [both * x - on_b * y for x, y in zip(a, b)]
    return [fa, [-x - y for x, y in zip(fa, fb)], fb]


def torsion_push(p0, p1, p2, p3):
    one = minus(p1, p0)
    two = minus(p2, p1)
    three = minus(p3, p2)
    m = cross3(one, two)
    n = cross3(two, three)
    im = lax.rsqrt(dot3(m, m) + 0.1)
    in_ = lax.rsqrt(dot3(n, n) + 0.1)
    both = -TORSION_K * (im * in_)
    dih = dot3(m, n) * both
    cm = dih * (im * im)
    cn = dih * (in_ * in_)
    gm = [both * y - cm * x for x, y in zip(m, n)]
    gn = [both * x - cn * y for x, y in zip(m, n)]
    f_one = cross3(two, gm)
    f_three = cross3(gn, two)
    f_two = [x + y for x, y in zip(cross3(gm, one), cross3(three, gn))]
    return [
        [-x for x in f_one],
        minus(f_one, f_two),
        minus(f_two, f_three),
        f_three,
    ]


def split3(x):
    top = x.astype(jnp.bfloat16)
    rest = x - top.astype(jnp.float32)
    mid = rest.astype(jnp.bfloat16)
    low = (rest - mid.astype(jnp.float32)).astype(jnp.bfloat16)
    return jnp.concatenate([top, mid, low], axis=0)


def merge3(x):
    n = x.shape[0] // 3
    return x[0:n] + x[n : 2 * n] + x[2 * n : 3 * n]


def final_kernel(
    count,
    high,
    part_ref,
    both_ref,
    dip_ref,
    quad_ref,
    x_out,
    v_out,
    f_out,
    t_out,
    land_ref,
    force_ref,
    lo_ref,
    hi_ref,
    send_sem,
    recv_sem,
    force_send,
    force_recv,
):
    half = count // 2
    width = f_out.shape[1]
    chunks = width // LANES
    used = 2 * chunks
    place = my_place()
    sub = lax.axis_index("sub")
    greet(half, place, count)

    def copy(j):
        return pltpu.make_async_remote_copy(
            src_ref=part_ref.at[:, pl.ds(pl.multiple_of(j * width, LANES), width)],
            dst_ref=land_ref.at[j],
            send_sem=send_sem.at[j],
            recv_sem=recv_sem.at[j],
            device_id=device_at((place + j) % count),
            device_id_type=MESH,
        )

    def start(j, _):
        copy(j).start()
        return 0

    def finish_one(j, total):
        copy(j).wait()
        return total + land_ref[j]

    lax.fori_loop(1, half + 1, start, 0)

    rows = both_ref.shape[1]
    n_mult = (rows - 10) // 7
    n_bond = 2 * width
    n_term = n_mult * n_bond
    total_terms = 2 * n_bond + 7 * n_term
    index = jnp.concatenate(
        [both_ref[k, row : row + 1, :] for row in range(8, rows) for k in range(2)], axis=1
    ).astype(jnp.int32)
    hi_part = index // LANES
    lo_part = index - hi_part * LANES
    lo_rows = lax.broadcasted_iota(jnp.int32, (LANES, total_terms), 0)
    lo_ref[...] = jnp.where(lo_rows == lo_part, 1.0, 0.0).astype(jnp.bfloat16)
    hi_rows = lax.broadcasted_iota(jnp.int32, (high, total_terms), 0)
    hi_ref[...] = jnp.where(hi_rows == hi_part, 1.0, 0.0)
    rest = jnp.concatenate([both_ref[k, 7:8, :] for k in range(2)], axis=1)
    fill = [jnp.zeros((high - used, LANES), jnp.float32)] if high > used else []

    def tiled(read, wanted):
        pieces = []
        for row in wanted:
            for k in range(2):
                for c in range(chunks):
                    pieces.append(read(k, row, c * LANES))
            pieces += fill
        return jnp.concatenate(pieces, axis=0)

    def from_pack(k, row, at):
        return both_ref[k, row : row + 1, at : at + LANES]

    def from_force(k, row, at):
        return force_ref[k, row : row + 1, at : at + LANES]

    mass = tiled(from_pack, (6, 6, 6))

    def push_at(coords):
        looked = merge3(
            jnp.dot(split3(coords), lo_ref[...], preferred_element_type=jnp.float32)
        )
        hi = hi_ref[...]
        row = [
            jnp.sum(looked[c * high : (c + 1) * high] * hi, axis=0, keepdims=True)
            for c in range(3)
        ]
        cuts = [(0, n_bond), (n_bond, 2 * n_bond)]
        cuts += [(2 * n_bond + j * n_term, 2 * n_bond + (j + 1) * n_term) for j in range(7)]
        atoms = [[row[c][:, lo:up] for c in range(3)] for lo, up in cuts]
        pushes = (
            bond_push(atoms[0], atoms[1], rest)
            + angle_push(*atoms[2:5])
            + torsion_push(*atoms[5:9])
        )
        spread = jnp.concatenate(
            [jnp.concatenate([p[c] for p in pushes], axis=1) * hi for c in range(3)], axis=0
        )
        return merge3(
            lax.dot_general(
                split3(spread),
                lo_ref[...],
                (((1,), (1,)), ((), ())),
                preferred_element_type=jnp.float32,
            )
        )

    dt = OUTER_DT / INNER
    x = tiled(from_pack, (0, 1, 2))
    half_step = (0.5 * dt) * mass
    v = tiled(from_pack, (3, 4, 5)) + half_step * push_at(x)

    total = lax.fori_loop(1, half + 1, finish_one, part_ref[:, 0:width])
    force_ref[sub] = total
    f_out[...] = total[0:3]
    swap = pltpu.make_async_remote_copy(
        src_ref=force_ref.at[sub],
        dst_ref=force_ref.at[sub],
        send_sem=force_send,
        recv_sem=force_recv,
        device_id=device_at(place + 1 - 2 * sub),
        device_id_type=MESH,
    )
    swap.start()
    t_out[...] = torque_of(
        [total[c : c + 1] for c in range(12)],
        [dip_ref[c : c + 1, :] for c in range(3)],
        [quad_ref[c : c + 1, :] for c in range(6)],
    )
    swap.wait()
    v = v + (0.5 * OUTER_DT) * tiled(from_force, (0, 1, 2)) * mass

    def substep(step, carry):
        x, v = carry
        x = x + dt * v
        kick = half_step * push_at(x)
        v = v + kick
        v = v + jnp.where(step < INNER - 1, kick, 0.0)
        return x, v

    x, v = lax.fori_loop(0, INNER, substep, (x, v))

    def mine(state):
        rows = []
        for c in range(3):
            sides = [
                jnp.concatenate(
                    [
                        state[c * high + k * chunks + h : c * high + k * chunks + h + 1]
                        for h in range(chunks)
                    ],
                    axis=1,
                )
                for k in range(2)
            ]
            rows.append(jnp.where(sub == 0, sides[0], sides[1]))
        return jnp.concatenate(rows, axis=0)

    x_out[...] = mine(x)
    v_out[...] = mine(v)


def body(
    positions,
    velocities,
    charges,
    dipoles,
    quadrupoles,
    damping,
    inverse_mass,
    bonds,
    bond_length,
    angles,
    torsions,
):
    atoms = positions.shape[1]
    n_sub = lax.axis_size("sub")
    record = jnp.concatenate(
        [positions, charges[None, :], dipoles, quadrupoles, damping[None, :]], 0
    )
    padded = jnp.concatenate([record, jnp.zeros((2, atoms), jnp.float32)], 0)
    own = padded.T
    count = lax.axis_size("blk") * lax.axis_size("rep") * n_sub
    slots = count // 2 + 1
    vmem = pl.BlockSpec(memory_space=pltpu.VMEM)
    dma = pltpu.SemaphoreType.DMA
    indices = jnp.concatenate(
        [bonds, angles.reshape(-1, atoms), torsions.reshape(-1, atoms)], 0
    )
    pack = jnp.concatenate(
        [
            positions,
            velocities,
            inverse_mass[None, :],
            bond_length[None, :],
            indices.astype(jnp.float32),
        ],
        0,
    )

    def params(**more):
        return pltpu.CompilerParams(vmem_limit_bytes=48 * 1024 * 1024, **more)

    def shape(*dims):
        return jax.ShapeDtypeStruct(dims, jnp.float32)

    everyone, both = pl.pallas_call(
        functools.partial(gather_kernel, count),
        out_shape=(shape(16, slots * atoms), shape(2, *pack.shape)),
        in_specs=[vmem] * 2,
        out_specs=(vmem, vmem),
        scratch_shapes=[dma((slots,)), dma((slots,)), dma, dma],
        compiler_params=params(collective_id=1),
        name="gather",
    )(padded, pack)
    parts = pl.pallas_call(
        functools.partial(pair_kernel, count),
        out_shape=shape(16, slots * atoms),
        in_specs=[vmem, vmem],
        out_specs=vmem,
        scratch_shapes=[
            pltpu.VMEM((96, slots * atoms), jnp.float32),
            pltpu.VMEM((atoms, LANES), jnp.float32),
        ],
        compiler_params=params(),
        name="pairs",
    )(own, everyone)
    high = -(-(n_sub * atoms // LANES) // 8) * 8
    total = n_sub * indices.shape[0] * atoms
    return pl.pallas_call(
        functools.partial(final_kernel, count, high),
        out_shape=(shape(3, atoms),) * 4,
        in_specs=[vmem] * 4,
        out_specs=(vmem,) * 4,
        scratch_shapes=[
            pltpu.VMEM((slots, 16, atoms), jnp.float32),
            pltpu.VMEM((2, 16, atoms), jnp.float32),
            pltpu.VMEM((LANES, total), jnp.bfloat16),
            pltpu.VMEM((high, total), jnp.float32),
            dma((slots,)),
            dma((slots,)),
            dma,
            dma,
        ],
        compiler_params=params(collective_id=2),
        name="finale",
    )(parts, both, dipoles, quadrupoles)


def solution(mesh):
    placed = (
        P(None, ("groups", "blk", "rep", "sub")),
        P(None, ("groups", "blk", "rep", "sub")),
        P(("groups", "blk", "rep", "sub")),
        P(None, ("groups", "blk", "rep", "sub")),
        P(None, ("groups", "blk", "rep", "sub")),
        P(("groups", "blk", "rep", "sub")),
        P(("groups", "blk", "rep", "sub")),
        P(None, ("groups", "blk", "rep", "sub")),
        P(("groups", "blk", "rep", "sub")),
        P(None, ("groups", "blk", "rep", "sub")),
        P(None, ("groups", "blk", "rep", "sub")),
    )
    return jax.shard_map(
        body,
        mesh=mesh,
        in_specs=placed,
        out_specs=(
            P(None, ("groups", "blk", "rep", "sub")),
            P(None, ("groups", "blk", "rep", "sub")),
            P(None, ("groups", "blk", "rep", "sub")),
            P(None, ("groups", "blk", "rep", "sub")),
        ),
        check_vma=False,
    )
```

```python
import functools

import jax
import jax.numpy as jnp
from jax import lax
from jax.experimental import pallas as pl
from jax.experimental.pallas import tpu as pltpu
from jax.sharding import PartitionSpec as P

INNER = 4
MESH = pl.DeviceIdType.MESH
LANES = 128
QUAD_INDEX = ((0, 1, 2), (1, 3, 4), (2, 4, 5))
BOND_K = 0.3
ANGLE_K = 4.0
ANGLE_REST = -0.33
TORSION_K = 2.0
OUTER_DT = 0.2
UNROLL = 3


def dot3(left, right):
    return left[0] * right[0] + left[1] * right[1] + left[2] * right[2]


def matvec(quad, vec):
    return [dot3([quad[QUAD_INDEX[a][b]] for b in range(3)], vec) for a in range(3)]


def my_place():
    n_rep = lax.axis_size("rep")
    n_sub = lax.axis_size("sub")
    return (lax.axis_index("blk") * n_rep + lax.axis_index("rep")) * n_sub + lax.axis_index("sub")


def device_at(place):
    n_rep = lax.axis_size("rep")
    n_sub = lax.axis_size("sub")
    return (
        lax.axis_index("groups"),
        place // (n_rep * n_sub),
        (place // n_sub) % n_rep,
        place % n_sub,
    )


def greet(half, place, count):
    barrier = pltpu.get_barrier_semaphore()

    def one(j, _):
        for other in ((place + j) % count, (place + count - j) % count):
            pl.semaphore_signal(
                barrier, inc=1, device_id=device_at(other), device_id_type=MESH
            )
        return 0

    lax.fori_loop(1, half + 1, one, 0)
    pl.semaphore_wait(barrier, 2 * half)


def gather_kernel(
    count,
    pos_any,
    vel_any,
    dip_any,
    quad_any,
    scal_ref,
    bond_any,
    angle_any,
    torsion_any,
    out_ref,
    both_ref,
    own_ref,
    near_ref,
    pos_ref,
    vel_ref,
    dip_ref,
    quad_ref,
    bond_ref,
    angle_ref,
    torsion_ref,
    record_ref,
    pack_ref,
    local_sem,
    send_sem,
    recv_sem,
    pack_send,
    pack_recv,
):
    half = count // 2
    width = pos_any.shape[1]
    place = my_place()
    sub = lax.axis_index("sub")
    loads = [
        pltpu.make_async_copy(src, dst, local_sem.at[n])
        for n, (src, dst) in enumerate(
            (
                (pos_any, pos_ref),
                (vel_any, vel_ref),
                (dip_any, dip_ref),
                (quad_any, quad_ref),
                (bond_any, bond_ref),
                (angle_any, angle_ref),
                (torsion_any, torsion_ref),
            )
        )
    ]
    for load in loads:
        load.start()
    greet(half, place, count)
    for load in loads:
        load.wait()

    record_ref[...] = jnp.concatenate(
        [
            pos_ref[...],
            scal_ref[0:1, :],
            dip_ref[...],
            quad_ref[...],
            scal_ref[1:2, :],
            jnp.zeros((2, width), jnp.float32),
        ],
        axis=0,
    )

    def copy(j):
        return pltpu.make_async_remote_copy(
            src_ref=record_ref,
            dst_ref=out_ref.at[:, pl.ds(pl.multiple_of(j * width, LANES), width)],
            send_sem=send_sem.at[j],
            recv_sem=recv_sem.at[j],
            device_id=device_at((place + count - j) % count),
            device_id_type=MESH,
        )

    def start(j, _):
        copy(j).start()
        return 0

    def finish_one(j, _):
        copy(j).wait()
        return 0

    lax.fori_loop(1, half + 1, start, 0)

    def cut(ref):
        whole = ref[...].astype(jnp.float32)
        return [
            whole[row : row + 1, at : at + width]
            for row in range(whole.shape[0])
            for at in range(0, whole.shape[1], width)
        ]

    pack_ref[...] = jnp.concatenate(
        [pos_ref[...], vel_ref[...], scal_ref[2:4, :]]
        + cut(bond_ref)
        + cut(angle_ref)
        + cut(torsion_ref),
        axis=0,
    )
    swap = pltpu.make_async_remote_copy(
        src_ref=pack_ref,
        dst_ref=both_ref.at[sub],
        send_sem=pack_send,
        recv_sem=pack_recv,
        device_id=device_at(place + 1 - 2 * sub),
        device_id_type=MESH,
    )
    swap.start()
    out_ref[:, 0:width] = record_ref[...]
    both_ref[sub] = pack_ref[...]
    wide = jnp.concatenate([record_ref[...], jnp.zeros((LANES - 16, width), jnp.float32)], axis=0)
    chunks = width // LANES
    for c in range(chunks):
        own_ref[c * LANES : (c + 1) * LANES, :] = wide[:, c * LANES : (c + 1) * LANES].T
    lane = lax.broadcasted_iota(jnp.int32, (8, LANES), 1)
    sublane = lax.broadcasted_iota(jnp.int32, (8, LANES), 0)
    diff = lane - sublane

    def one_group(group, _):
        base = pl.multiple_of(group * 8, 8)
        target = [
            jnp.broadcast_to(own_ref[pl.ds(base, 8), c : c + 1], (8, LANES)) for c in range(14)
        ]

        def near(chunk, sums):
            at = pl.multiple_of(chunk * LANES, LANES)
            source = [record_ref[c : c + 1, pl.ds(at, LANES)] for c in range(14)]

            def alive(root):
                return jnp.where(diff == base - at, 0.0, root)

            push, on_i, _ = pair_terms(target, source, alive)
            return tuple(x + y for x, y in zip(sums, push + on_i))

        sums = lax.fori_loop(0, chunks, near, (jnp.zeros((8, LANES), jnp.float32),) * 12)
        near_ref[pl.ds(base, 8), :] = row_sums(sums)
        return 0

    lax.fori_loop(0, width // 8, one_group, 0)
    swap.wait()
    lax.fori_loop(1, half + 1, finish_one, 0)


def row_sums(sums):
    return jnp.concatenate(
        [jnp.sum(x, axis=1, keepdims=True) for x in sums]
        + [jnp.zeros((8, LANES - len(sums)), jnp.float32)],
        axis=1,
    )


def pair_terms(target, source, alive):
    c_i, d_i, q_i = target[3], target[4:7], target[7:13]
    c_k, d_k, q_k = source[3], source[4:7], source[7:13]
    r = [source[c] - target[c] for c in range(3)]
    s = dot3(r, r) + target[13] * source[13]
    root = lax.rsqrt(s)
    b1 = alive(root)
    inv = root * root
    b3 = b1 * inv
    b5 = b3 * (3.0 * inv)
    b7 = b5 * (5.0 * inv)
    b9 = b7 * (7.0 * inv)
    b11 = b9 * (9.0 * inv)
    f5 = 2.0 * b5
    f7 = 4.0 * b7
    f10 = 4.0 * b5
    w = matvec(q_k, r)
    u = matvec(q_i, r)
    dk = dot3(d_k, r)
    qk = dot3(w, r)
    di = dot3(d_i, r)
    qi = dot3(u, r)
    a_i = c_k * b3 - dk * b5 + qk * b7
    b_i = c_k * b5 - dk * b7 + qk * b9
    g_i = c_k * b7 - dk * b9 + qk * b11
    a_k = c_i * b3 + di * b5 + qi * b7
    b_k = c_i * b5 + di * b7 + qi * b9
    h_i = [f5 * d_k[a] - f7 * w[a] for a in range(3)]
    h_k = [f5 * d_i[a] + f7 * u[a] for a in range(3)]
    br_i = [b_i * r[a] for a in range(3)]
    br_k = [b_k * r[a] for a in range(3)]
    v_i = [br_i[a] + h_i[a] for a in range(3)]
    v_k = [br_k[a] - h_k[a] for a in range(3)]
    on_i = matvec(q_i, [v_i[a] + br_i[a] for a in range(3)])
    on_k = matvec(q_k, [v_k[a] + br_k[a] for a in range(3)])
    qm = (q_i[0] * q_k[0] + q_i[3] * q_k[3] + q_i[5] * q_k[5]) + 2.0 * (
        q_i[1] * q_k[1] + q_i[2] * q_k[2] + q_i[4] * q_k[4]
    )
    alpha = (
        c_i * a_i
        + di * b_i
        + qi * g_i
        + 0.5 * (dot3(d_i, h_i) + f7 * (dot3(d_k, u) + qm))
        - (4.0 * b9) * dot3(u, w)
    )
    push = [
        (a_i * d_i[a] - a_k * d_k[a]) + (on_i[a] + on_k[a]) - alpha * r[a] for a in range(3)
    ]

    def quad_rows(v, q):
        return [
            r[0] * v[0] + f5 * q[0],
            (r[0] * v[1] + r[1] * v[0]) + f10 * q[1],
            (r[0] * v[2] + r[2] * v[0]) + f10 * q[2],
            r[1] * v[1] + f5 * q[3],
            (r[1] * v[2] + r[2] * v[1]) + f10 * q[4],
            r[2] * v[2] + f5 * q[5],
        ]

    f_i = [a_i * r[a] + b3 * d_k[a] - f5 * w[a] for a in range(3)]
    f_k = [b3 * d_i[a] + f5 * u[a] - a_k * r[a] for a in range(3)]
    return push, f_i + quad_rows(v_i, q_k), f_k + quad_rows(v_k, q_i)


def pair_kernel(count, own_ref, near_ref, all_ref, out_ref, acc_ref, tgt_ref):
    half = count // 2
    rows = own_ref.shape[0]
    chunks = rows // LANES
    lower = my_place() < half
    acc_ref[...] = jnp.zeros_like(acc_ref)
    zero = jnp.zeros((8, LANES), jnp.float32)

    def source_at(start):
        return [all_ref[c : c + 1, pl.ds(start, LANES)] for c in range(14)]

    def one_group(group, _):
        base = pl.multiple_of(group * 8, 8)
        target = [
            jnp.broadcast_to(own_ref[pl.ds(base, 8), c : c + 1], (8, LANES)) for c in range(14)
        ]

        def far(chunk, sums):
            start = pl.multiple_of(chunk * LANES, LANES)
            push, on_i, on_k = pair_terms(target, source_at(start), lambda root: root)
            for c in range(3):
                acc_ref[8 * c : 8 * c + 8, pl.ds(start, LANES)] -= push[c]
            for c in range(9):
                acc_ref[24 + 8 * c : 32 + 8 * c, pl.ds(start, LANES)] += on_k[c]
            return tuple(x + y for x, y in zip(sums, push + on_i))

        first = lax.rem(base // LANES + jnp.where(lower, 0, 1), 2)

        def last(step, sums):
            return far(half * chunks + first + 2 * step, sums)

        sums = lax.fori_loop(chunks, half * chunks, far, (zero,) * 12, unroll=UNROLL)
        sums = lax.fori_loop(0, (chunks - first + 1) // 2, last, sums)
        tgt_ref[pl.ds(base, 8), :] = near_ref[pl.ds(base, 8), :] + row_sums(sums)
        return 0

    lax.fori_loop(0, rows // 8, one_group, 0)

    def fold(chunk, _):
        at = pl.ds(pl.multiple_of(chunk * LANES, LANES), LANES)
        out_ref[:, at] = jnp.concatenate(
            [jnp.sum(acc_ref[8 * c : 8 * c + 8, at], axis=0, keepdims=True) for c in range(12)]
            + [jnp.zeros((4, LANES), jnp.float32)],
            axis=0,
        )
        return 0

    lax.fori_loop(chunks, (half + 1) * chunks, fold, 0)
    for c in range(chunks):
        flipped = tgt_ref[c * LANES : (c + 1) * LANES, :].T
        out_ref[:, c * LANES : (c + 1) * LANES] = flipped[0:16]


def torque_of(sums, d, q):
    field = [-sums[3 + a] for a in range(3)]
    halves = (1.0, 0.5, 0.5, 1.0, 0.5, 1.0)
    g = [halves[c] * sums[6 + c] for c in range(6)]

    def product(a, b):
        return dot3(
            [q[QUAD_INDEX[a][c]] for c in range(3)], [g[QUAD_INDEX[c][b]] for c in range(3)]
        )

    return jnp.concatenate(
        [
            d[1] * field[2] - d[2] * field[1] - 2.0 * (product(1, 2) - product(2, 1)),
            d[2] * field[0] - d[0] * field[2] - 2.0 * (product(2, 0) - product(0, 2)),
            d[0] * field[1] - d[1] * field[0] - 2.0 * (product(0, 1) - product(1, 0)),
        ],
        axis=0,
    )


def cross3(a, b):
    return [
        a[1] * b[2] - a[2] * b[1],
        a[2] * b[0] - a[0] * b[2],
        a[0] * b[1] - a[1] * b[0],
    ]


def minus(a, b):
    return [x - y for x, y in zip(a, b)]


def bond_push(first, second, rest):
    step = minus(second, first)
    sq = dot3(step, step) + 0.01
    scale = BOND_K * (1.0 - rest * lax.rsqrt(sq))
    pull = [scale * x for x in step]
    return [pull, [-x for x in pull]]


def angle_push(first, centre, third):
    a = minus(first, centre)
    b = minus(third, centre)
    ia = lax.rsqrt(dot3(a, a) + 0.01)
    ib = lax.rsqrt(dot3(b, b) + 0.01)
    cosine = dot3(a, b) * (ia * ib)
    lead = -ANGLE_K * (cosine - ANGLE_REST)
    both = lead * (ia * ib)
    on_a = lead * cosine * (ia * ia)
    on_b = lead * cosine * (ib * ib)
    fa = [both * y - on_a * x for x, y in zip(a, b)]
    fb = [both * x - on_b * y for x, y in zip(a, b)]
    return [fa, [-x - y for x, y in zip(fa, fb)], fb]


def torsion_push(p0, p1, p2, p3):
    one = minus(p1, p0)
    two = minus(p2, p1)
    three = minus(p3, p2)
    m = cross3(one, two)
    n = cross3(two, three)
    im = lax.rsqrt(dot3(m, m) + 0.1)
    in_ = lax.rsqrt(dot3(n, n) + 0.1)
    both = -TORSION_K * (im * in_)
    dih = dot3(m, n) * both
    cm = dih * (im * im)
    cn = dih * (in_ * in_)
    gm = [both * y - cm * x for x, y in zip(m, n)]
    gn = [both * x - cn * y for x, y in zip(m, n)]
    f_one = cross3(two, gm)
    f_three = cross3(gn, two)
    f_two = [x + y for x, y in zip(cross3(gm, one), cross3(three, gn))]
    return [
        [-x for x in f_one],
        minus(f_one, f_two),
        minus(f_two, f_three),
        f_three,
    ]


def split3(x):
    top = x.astype(jnp.bfloat16)
    rest = x - top.astype(jnp.float32)
    mid = rest.astype(jnp.bfloat16)
    low = (rest - mid.astype(jnp.float32)).astype(jnp.bfloat16)
    return jnp.concatenate([top, mid, low], axis=0)


def merge3(x):
    n = x.shape[0] // 3
    return x[0:n] + x[n : 2 * n] + x[2 * n : 3 * n]


def final_kernel(
    count,
    high,
    part_ref,
    both_ref,
    all_ref,
    out_ref,
    land_ref,
    force_ref,
    lo_ref,
    hi_ref,
    send_sem,
    recv_sem,
    force_send,
    force_recv,
):
    half = count // 2
    width = out_ref.shape[1]
    chunks = width // LANES
    used = 2 * chunks
    place = my_place()
    sub = lax.axis_index("sub")
    greet(half, place, count)

    def copy(j):
        return pltpu.make_async_remote_copy(
            src_ref=part_ref.at[:, pl.ds(pl.multiple_of(j * width, LANES), width)],
            dst_ref=land_ref.at[j],
            send_sem=send_sem.at[j],
            recv_sem=recv_sem.at[j],
            device_id=device_at((place + j) % count),
            device_id_type=MESH,
        )

    def start(j, _):
        copy(j).start()
        return 0

    def finish_one(j, total):
        copy(j).wait()
        return total + land_ref[j]

    lax.fori_loop(1, half + 1, start, 0)

    rows = both_ref.shape[1]
    n_mult = (rows - 10) // 7
    n_bond = 2 * width
    n_term = n_mult * n_bond
    total_terms = 2 * n_bond + 7 * n_term
    index = jnp.concatenate(
        [both_ref[k, row : row + 1, :] for row in range(8, rows) for k in range(2)], axis=1
    ).astype(jnp.int32)
    hi_part = index // LANES
    lo_part = index - hi_part * LANES
    lo_rows = lax.broadcasted_iota(jnp.int32, (LANES, total_terms), 0)
    lo_ref[...] = jnp.where(lo_rows == lo_part, 1.0, 0.0).astype(jnp.bfloat16)
    hi_rows = lax.broadcasted_iota(jnp.int32, (high, total_terms), 0)
    hi_ref[...] = jnp.where(hi_rows == hi_part, 1.0, 0.0)
    rest = jnp.concatenate([both_ref[k, 7:8, :] for k in range(2)], axis=1)
    fill = [jnp.zeros((high - used, LANES), jnp.float32)] if high > used else []

    def tiled(read, wanted):
        pieces = []
        for row in wanted:
            for k in range(2):
                for c in range(chunks):
                    pieces.append(read(k, row, c * LANES))
            pieces += fill
        return jnp.concatenate(pieces, axis=0)

    def from_pack(k, row, at):
        return both_ref[k, row : row + 1, at : at + LANES]

    def from_force(k, row, at):
        return force_ref[k, row : row + 1, at : at + LANES]

    mass = tiled(from_pack, (6, 6, 6))

    def push_at(coords):
        looked = merge3(
            jnp.dot(split3(coords), lo_ref[...], preferred_element_type=jnp.float32)
        )
        hi = hi_ref[...]
        row = [
            jnp.sum(looked[c * high : (c + 1) * high] * hi, axis=0, keepdims=True)
            for c in range(3)
        ]
        cuts = [(0, n_bond), (n_bond, 2 * n_bond)]
        cuts += [(2 * n_bond + j * n_term, 2 * n_bond + (j + 1) * n_term) for j in range(7)]
        atoms = [[row[c][:, lo:up] for c in range(3)] for lo, up in cuts]
        pushes = (
            bond_push(atoms[0], atoms[1], rest)
            + angle_push(*atoms[2:5])
            + torsion_push(*atoms[5:9])
        )
        spread = jnp.concatenate(
            [jnp.concatenate([p[c] for p in pushes], axis=1) * hi for c in range(3)], axis=0
        )
        return merge3(
            lax.dot_general(
                split3(spread),
                lo_ref[...],
                (((1,), (1,)), ((), ())),
                preferred_element_type=jnp.float32,
            )
        )

    dt = OUTER_DT / INNER
    x = tiled(from_pack, (0, 1, 2))
    half_step = (0.5 * dt) * mass
    v = tiled(from_pack, (3, 4, 5)) + half_step * push_at(x)

    total = lax.fori_loop(1, half + 1, finish_one, part_ref[:, 0:width])
    force_ref[sub] = total
    swap = pltpu.make_async_remote_copy(
        src_ref=force_ref.at[sub],
        dst_ref=force_ref.at[sub],
        send_sem=force_send,
        recv_sem=force_recv,
        device_id=device_at(place + 1 - 2 * sub),
        device_id_type=MESH,
    )
    swap.start()
    torque = torque_of(
        [total[c : c + 1] for c in range(12)],
        [all_ref[c : c + 1, 0:width] for c in range(4, 7)],
        [all_ref[c : c + 1, 0:width] for c in range(7, 13)],
    )
    swap.wait()
    v = v + (0.5 * OUTER_DT) * tiled(from_force, (0, 1, 2)) * mass

    def substep(step, carry):
        x, v = carry
        x = x + dt * v
        kick = half_step * push_at(x)
        v = v + kick
        v = v + jnp.where(step < INNER - 1, kick, 0.0)
        return x, v

    x, v = lax.fori_loop(0, INNER, substep, (x, v))

    def mine(state):
        rows = []
        for c in range(3):
            sides = [
                jnp.concatenate(
                    [
                        state[c * high + k * chunks + h : c * high + k * chunks + h + 1]
                        for h in range(chunks)
                    ],
                    axis=1,
                )
                for k in range(2)
            ]
            rows.append(jnp.where(sub == 0, sides[0], sides[1]))
        return jnp.concatenate(rows, axis=0)

    out_ref[...] = jnp.concatenate([mine(x), mine(v), total[0:3], torque], axis=0)


def body(
    positions,
    velocities,
    charges,
    dipoles,
    quadrupoles,
    damping,
    inverse_mass,
    bonds,
    bond_length,
    angles,
    torsions,
):
    atoms = positions.shape[1]
    n_sub = lax.axis_size("sub")
    count = lax.axis_size("blk") * lax.axis_size("rep") * n_sub
    slots = count // 2 + 1
    vmem = pl.BlockSpec(memory_space=pltpu.VMEM)
    dma = pltpu.SemaphoreType.DMA
    hbm = pl.BlockSpec(memory_space=pl.ANY)
    scalars = jnp.stack([charges, damping, inverse_mass, bond_length])
    index_rows = 2 + (angles.size + torsions.size) // atoms
    pack_rows = 8 + index_rows

    def params(**more):
        return pltpu.CompilerParams(vmem_limit_bytes=48 * 1024 * 1024, **more)

    def shape(*dims):
        return jax.ShapeDtypeStruct(dims, jnp.float32)

    everyone, both, own, near = pl.pallas_call(
        functools.partial(gather_kernel, count),
        out_shape=(
            shape(16, slots * atoms),
            shape(2, pack_rows, atoms),
            shape(atoms, LANES),
            shape(atoms, LANES),
        ),
        in_specs=[hbm] * 4 + [vmem] + [hbm] * 3,
        out_specs=(vmem,) * 4,
        scratch_shapes=[
            pltpu.VMEM(x.shape, x.dtype)
            for x in (positions, velocities, dipoles, quadrupoles, bonds, angles, torsions)
        ]
        + [
            pltpu.VMEM((16, atoms), jnp.float32),
            pltpu.VMEM((pack_rows, atoms), jnp.float32),
            dma((7,)),
            dma((slots,)),
            dma((slots,)),
            dma,
            dma,
        ],
        compiler_params=params(collective_id=1),
        name="gather",
    )(positions, velocities, dipoles, quadrupoles, scalars, bonds, angles, torsions)
    parts = pl.pallas_call(
        functools.partial(pair_kernel, count),
        out_shape=shape(16, slots * atoms),
        in_specs=[vmem] * 3,
        out_specs=vmem,
        scratch_shapes=[
            pltpu.VMEM((96, slots * atoms), jnp.float32),
            pltpu.VMEM((atoms, LANES), jnp.float32),
        ],
        compiler_params=params(),
        name="pairs",
    )(own, near, everyone)
    high = -(-(n_sub * atoms // LANES) // 8) * 8
    total = n_sub * index_rows * atoms
    out = pl.pallas_call(
        functools.partial(final_kernel, count, high),
        out_shape=shape(12, atoms),
        in_specs=[vmem] * 3,
        out_specs=vmem,
        scratch_shapes=[
            pltpu.VMEM((slots, 16, atoms), jnp.float32),
            pltpu.VMEM((2, 16, atoms), jnp.float32),
            pltpu.VMEM((LANES, total), jnp.bfloat16),
            pltpu.VMEM((high, total), jnp.float32),
            dma((slots,)),
            dma((slots,)),
            dma,
            dma,
        ],
        compiler_params=params(collective_id=2),
        name="finale",
    )(parts, both, everyone)
    return tuple(out[3 * n : 3 * n + 3] for n in range(4))


def solution(mesh):
    placed = (
        P(None, ("groups", "blk", "rep", "sub")),
        P(None, ("groups", "blk", "rep", "sub")),
        P(("groups", "blk", "rep", "sub")),
        P(None, ("groups", "blk", "rep", "sub")),
        P(None, ("groups", "blk", "rep", "sub")),
        P(("groups", "blk", "rep", "sub")),
        P(("groups", "blk", "rep", "sub")),
        P(None, ("groups", "blk", "rep", "sub")),
        P(("groups", "blk", "rep", "sub")),
        P(None, ("groups", "blk", "rep", "sub")),
        P(None, ("groups", "blk", "rep", "sub")),
    )
    return jax.shard_map(
        body,
        mesh=mesh,
        in_specs=placed,
        out_specs=(
            P(None, ("groups", "blk", "rep", "sub")),
            P(None, ("groups", "blk", "rep", "sub")),
            P(None, ("groups", "blk", "rep", "sub")),
            P(None, ("groups", "blk", "rep", "sub")),
        ),
        check_vma=False,
    )
```

```python
import functools

import jax
import jax.numpy as jnp
from jax import lax
from jax.experimental import pallas as pl
from jax.experimental.pallas import tpu as pltpu
from jax.sharding import PartitionSpec as P

INNER = 4
MESH = pl.DeviceIdType.MESH
LANES = 128
QUAD_INDEX = ((0, 1, 2), (1, 3, 4), (2, 4, 5))
BOND_K = 0.3
ANGLE_K = 4.0
ANGLE_REST = -0.33
TORSION_K = 2.0
OUTER_DT = 0.2
UNROLL = 3


def dot3(left, right):
    return left[0] * right[0] + left[1] * right[1] + left[2] * right[2]


def matvec(quad, vec):
    return [dot3([quad[QUAD_INDEX[a][b]] for b in range(3)], vec) for a in range(3)]


def my_place():
    n_rep = lax.axis_size("rep")
    n_sub = lax.axis_size("sub")
    return (lax.axis_index("blk") * n_rep + lax.axis_index("rep")) * n_sub + lax.axis_index("sub")


def device_at(place):
    n_rep = lax.axis_size("rep")
    n_sub = lax.axis_size("sub")
    return (
        lax.axis_index("groups"),
        place // (n_rep * n_sub),
        (place // n_sub) % n_rep,
        place % n_sub,
    )


def greet(half, place, count):
    barrier = pltpu.get_barrier_semaphore()

    def one(j, _):
        for other in ((place + j) % count, (place + count - j) % count):
            pl.semaphore_signal(
                barrier, inc=1, device_id=device_at(other), device_id_type=MESH
            )
        return 0

    lax.fori_loop(1, half + 1, one, 0)


def all_here(half):
    pl.semaphore_wait(pltpu.get_barrier_semaphore(), 2 * half)


def gather_kernel(
    count,
    pos_any,
    vel_any,
    dip_any,
    quad_any,
    scal_ref,
    bond_any,
    angle_any,
    torsion_any,
    out_ref,
    both_ref,
    own_ref,
    near_ref,
    pos_ref,
    vel_ref,
    dip_ref,
    quad_ref,
    bond_ref,
    angle_ref,
    torsion_ref,
    record_ref,
    pack_ref,
    local_sem,
    send_sem,
    recv_sem,
    pack_send,
    pack_recv,
):
    half = count // 2
    width = pos_any.shape[1]
    place = my_place()
    sub = lax.axis_index("sub")
    loads = [
        pltpu.make_async_copy(src, dst, local_sem.at[n])
        for n, (src, dst) in enumerate(
            (
                (pos_any, pos_ref),
                (vel_any, vel_ref),
                (dip_any, dip_ref),
                (quad_any, quad_ref),
                (bond_any, bond_ref),
                (angle_any, angle_ref),
                (torsion_any, torsion_ref),
            )
        )
    ]
    for load in loads:
        load.start()
    greet(half, place, count)
    for load in loads:
        load.wait()

    record_ref[...] = jnp.concatenate(
        [
            pos_ref[...],
            scal_ref[0:1, :],
            dip_ref[...],
            quad_ref[...],
            scal_ref[1:2, :],
            jnp.zeros((2, width), jnp.float32),
        ],
        axis=0,
    )

    def copy(j):
        return pltpu.make_async_remote_copy(
            src_ref=record_ref,
            dst_ref=out_ref.at[:, pl.ds(pl.multiple_of(j * width, LANES), width)],
            send_sem=send_sem.at[j],
            recv_sem=recv_sem.at[j],
            device_id=device_at((place + count - j) % count),
            device_id_type=MESH,
        )

    def start(j, _):
        copy(j).start()
        return 0

    def finish_one(j, _):
        copy(j).wait()
        return 0

    def cut(ref):
        whole = ref[...].astype(jnp.float32)
        return [
            whole[row : row + 1, at : at + width]
            for row in range(whole.shape[0])
            for at in range(0, whole.shape[1], width)
        ]

    pack_ref[...] = jnp.concatenate(
        [pos_ref[...], vel_ref[...], scal_ref[2:4, :]]
        + cut(bond_ref)
        + cut(angle_ref)
        + cut(torsion_ref),
        axis=0,
    )
    out_ref[:, 0:width] = record_ref[...]
    both_ref[sub] = pack_ref[...]
    wide = jnp.concatenate([record_ref[...], jnp.zeros((LANES - 16, width), jnp.float32)], axis=0)
    chunks = width // LANES
    for c in range(chunks):
        own_ref[c * LANES : (c + 1) * LANES, :] = wide[:, c * LANES : (c + 1) * LANES].T
    lane = lax.broadcasted_iota(jnp.int32, (8, LANES), 1)
    sublane = lax.broadcasted_iota(jnp.int32, (8, LANES), 0)
    diff = lane - sublane

    def one_group(group, _):
        base = pl.multiple_of(group * 8, 8)
        target = [
            jnp.broadcast_to(own_ref[pl.ds(base, 8), c : c + 1], (8, LANES)) for c in range(14)
        ]

        def near(chunk, sums):
            at = pl.multiple_of(chunk * LANES, LANES)
            source = [record_ref[c : c + 1, pl.ds(at, LANES)] for c in range(14)]

            def alive(root):
                return jnp.where(diff == base - at, 0.0, root)

            push, on_i, _ = pair_terms(target, source, alive)
            return tuple(x + y for x, y in zip(sums, push + on_i))

        sums = lax.fori_loop(0, chunks, near, (jnp.zeros((8, LANES), jnp.float32),) * 12, unroll=True)
        near_ref[pl.ds(base, 8), :] = row_sums(sums)
        return 0

    groups = width // 8
    early = groups // 3
    lax.fori_loop(0, early, one_group, 0)
    all_here(half)
    lax.fori_loop(1, half + 1, start, 0)
    swap = pltpu.make_async_remote_copy(
        src_ref=pack_ref,
        dst_ref=both_ref.at[sub],
        send_sem=pack_send,
        recv_sem=pack_recv,
        device_id=device_at(place + 1 - 2 * sub),
        device_id_type=MESH,
    )
    swap.start()
    lax.fori_loop(early, groups, one_group, 0)
    swap.wait()
    lax.fori_loop(1, half + 1, finish_one, 0)


def row_sums(sums):
    return jnp.concatenate(
        [jnp.sum(x, axis=1, keepdims=True) for x in sums]
        + [jnp.zeros((8, LANES - len(sums)), jnp.float32)],
        axis=1,
    )


def pair_terms(target, source, alive):
    c_i, d_i, q_i = target[3], target[4:7], target[7:13]
    c_k, d_k, q_k = source[3], source[4:7], source[7:13]
    r = [source[c] - target[c] for c in range(3)]
    s = dot3(r, r) + target[13] * source[13]
    root = lax.rsqrt(s)
    b1 = alive(root)
    inv = root * root
    b3 = b1 * inv
    b5 = b3 * (3.0 * inv)
    b7 = b5 * (5.0 * inv)
    b9 = b7 * (7.0 * inv)
    b11 = b9 * (9.0 * inv)
    f5 = 2.0 * b5
    f7 = 4.0 * b7
    f10 = 4.0 * b5
    w = matvec(q_k, r)
    u = matvec(q_i, r)
    dk = dot3(d_k, r)
    qk = dot3(w, r)
    di = dot3(d_i, r)
    qi = dot3(u, r)
    a_i = c_k * b3 - dk * b5 + qk * b7
    b_i = c_k * b5 - dk * b7 + qk * b9
    g_i = c_k * b7 - dk * b9 + qk * b11
    a_k = c_i * b3 + di * b5 + qi * b7
    b_k = c_i * b5 + di * b7 + qi * b9
    h_i = [f5 * d_k[a] - f7 * w[a] for a in range(3)]
    h_k = [f5 * d_i[a] + f7 * u[a] for a in range(3)]
    br_i = [b_i * r[a] for a in range(3)]
    br_k = [b_k * r[a] for a in range(3)]
    v_i = [br_i[a] + h_i[a] for a in range(3)]
    v_k = [br_k[a] - h_k[a] for a in range(3)]
    on_i = matvec(q_i, [v_i[a] + br_i[a] for a in range(3)])
    on_k = matvec(q_k, [v_k[a] + br_k[a] for a in range(3)])
    qm = (q_i[0] * q_k[0] + q_i[3] * q_k[3] + q_i[5] * q_k[5]) + 2.0 * (
        q_i[1] * q_k[1] + q_i[2] * q_k[2] + q_i[4] * q_k[4]
    )
    alpha = (
        c_i * a_i
        + di * b_i
        + qi * g_i
        + 0.5 * (dot3(d_i, h_i) + f7 * (dot3(d_k, u) + qm))
        - (4.0 * b9) * dot3(u, w)
    )
    push = [
        (a_i * d_i[a] - a_k * d_k[a]) + (on_i[a] + on_k[a]) - alpha * r[a] for a in range(3)
    ]

    def quad_rows(v, q):
        return [
            r[0] * v[0] + f5 * q[0],
            (r[0] * v[1] + r[1] * v[0]) + f10 * q[1],
            (r[0] * v[2] + r[2] * v[0]) + f10 * q[2],
            r[1] * v[1] + f5 * q[3],
            (r[1] * v[2] + r[2] * v[1]) + f10 * q[4],
            r[2] * v[2] + f5 * q[5],
        ]

    f_i = [a_i * r[a] + b3 * d_k[a] - f5 * w[a] for a in range(3)]
    f_k = [b3 * d_i[a] + f5 * u[a] - a_k * r[a] for a in range(3)]
    return push, f_i + quad_rows(v_i, q_k), f_k + quad_rows(v_k, q_i)


def pair_kernel(count, own_ref, near_ref, all_ref, out_ref, acc_ref, tgt_ref):
    half = count // 2
    rows = own_ref.shape[0]
    chunks = rows // LANES
    lower = my_place() < half
    acc_ref[...] = jnp.zeros_like(acc_ref)
    zero = jnp.zeros((8, LANES), jnp.float32)

    def source_at(start):
        return [all_ref[c : c + 1, pl.ds(start, LANES)] for c in range(14)]

    def one_group(group, _):
        base = pl.multiple_of(group * 8, 8)
        target = [
            jnp.broadcast_to(own_ref[pl.ds(base, 8), c : c + 1], (8, LANES)) for c in range(14)
        ]

        def far(chunk, sums):
            start = pl.multiple_of(chunk * LANES, LANES)
            push, on_i, on_k = pair_terms(target, source_at(start), lambda root: root)
            for c in range(3):
                acc_ref[8 * c : 8 * c + 8, pl.ds(start, LANES)] -= push[c]
            for c in range(9):
                acc_ref[24 + 8 * c : 32 + 8 * c, pl.ds(start, LANES)] += on_k[c]
            return tuple(x + y for x, y in zip(sums, push + on_i))

        first = lax.rem(base // LANES + jnp.where(lower, 0, 1), 2)

        def last(step, sums):
            return far(half * chunks + first + 2 * step, sums)

        sums = lax.fori_loop(chunks, half * chunks, far, (zero,) * 12, unroll=UNROLL)
        sums = lax.fori_loop(0, (chunks - first + 1) // 2, last, sums)
        tgt_ref[pl.ds(base, 8), :] = near_ref[pl.ds(base, 8), :] + row_sums(sums)
        return 0

    lax.fori_loop(0, rows // 8, one_group, 0)

    def fold(chunk, _):
        at = pl.ds(pl.multiple_of(chunk * LANES, LANES), LANES)
        out_ref[:, at] = jnp.concatenate(
            [jnp.sum(acc_ref[8 * c : 8 * c + 8, at], axis=0, keepdims=True) for c in range(12)]
            + [jnp.zeros((4, LANES), jnp.float32)],
            axis=0,
        )
        return 0

    lax.fori_loop(chunks, (half + 1) * chunks, fold, 0)
    for c in range(chunks):
        flipped = tgt_ref[c * LANES : (c + 1) * LANES, :].T
        out_ref[:, c * LANES : (c + 1) * LANES] = flipped[0:16]


def torque_of(sums, d, q):
    field = [-sums[3 + a] for a in range(3)]
    halves = (1.0, 0.5, 0.5, 1.0, 0.5, 1.0)
    g = [halves[c] * sums[6 + c] for c in range(6)]

    def product(a, b):
        return dot3(
            [q[QUAD_INDEX[a][c]] for c in range(3)], [g[QUAD_INDEX[c][b]] for c in range(3)]
        )

    return jnp.concatenate(
        [
            d[1] * field[2] - d[2] * field[1] - 2.0 * (product(1, 2) - product(2, 1)),
            d[2] * field[0] - d[0] * field[2] - 2.0 * (product(2, 0) - product(0, 2)),
            d[0] * field[1] - d[1] * field[0] - 2.0 * (product(0, 1) - product(1, 0)),
        ],
        axis=0,
    )


def cross3(a, b):
    return [
        a[1] * b[2] - a[2] * b[1],
        a[2] * b[0] - a[0] * b[2],
        a[0] * b[1] - a[1] * b[0],
    ]


def minus(a, b):
    return [x - y for x, y in zip(a, b)]


def bond_push(first, second, rest):
    step = minus(second, first)
    sq = dot3(step, step) + 0.01
    scale = BOND_K * (1.0 - rest * lax.rsqrt(sq))
    pull = [scale * x for x in step]
    return [pull, [-x for x in pull]]


def angle_push(first, centre, third):
    a = minus(first, centre)
    b = minus(third, centre)
    ia = lax.rsqrt(dot3(a, a) + 0.01)
    ib = lax.rsqrt(dot3(b, b) + 0.01)
    cosine = dot3(a, b) * (ia * ib)
    lead = -ANGLE_K * (cosine - ANGLE_REST)
    both = lead * (ia * ib)
    on_a = lead * cosine * (ia * ia)
    on_b = lead * cosine * (ib * ib)
    fa = [both * y - on_a * x for x, y in zip(a, b)]
    fb = [both * x - on_b * y for x, y in zip(a, b)]
    return [fa, [-x - y for x, y in zip(fa, fb)], fb]


def torsion_push(p0, p1, p2, p3):
    one = minus(p1, p0)
    two = minus(p2, p1)
    three = minus(p3, p2)
    m = cross3(one, two)
    n = cross3(two, three)
    im = lax.rsqrt(dot3(m, m) + 0.1)
    in_ = lax.rsqrt(dot3(n, n) + 0.1)
    both = -TORSION_K * (im * in_)
    dih = dot3(m, n) * both
    cm = dih * (im * im)
    cn = dih * (in_ * in_)
    gm = [both * y - cm * x for x, y in zip(m, n)]
    gn = [both * x - cn * y for x, y in zip(m, n)]
    f_one = cross3(two, gm)
    f_three = cross3(gn, two)
    f_two = [x + y for x, y in zip(cross3(gm, one), cross3(three, gn))]
    return [
        [-x for x in f_one],
        minus(f_one, f_two),
        minus(f_two, f_three),
        f_three,
    ]


def split3(x):
    top = x.astype(jnp.bfloat16)
    rest = x - top.astype(jnp.float32)
    mid = rest.astype(jnp.bfloat16)
    low = (rest - mid.astype(jnp.float32)).astype(jnp.bfloat16)
    return jnp.concatenate([top, mid, low], axis=0)


def merge3(x):
    n = x.shape[0] // 3
    return x[0:n] + x[n : 2 * n] + x[2 * n : 3 * n]


def final_kernel(
    count,
    high,
    part_ref,
    both_ref,
    all_ref,
    out_ref,
    land_ref,
    force_ref,
    lo_ref,
    hi_ref,
    send_sem,
    recv_sem,
    force_send,
    force_recv,
):
    half = count // 2
    width = out_ref.shape[1]
    chunks = width // LANES
    used = 2 * chunks
    place = my_place()
    sub = lax.axis_index("sub")
    greet(half, place, count)
    all_here(half)

    def copy(j):
        return pltpu.make_async_remote_copy(
            src_ref=part_ref.at[:, pl.ds(pl.multiple_of(j * width, LANES), width)],
            dst_ref=land_ref.at[j],
            send_sem=send_sem.at[j],
            recv_sem=recv_sem.at[j],
            device_id=device_at((place + j) % count),
            device_id_type=MESH,
        )

    def start(j, _):
        copy(j).start()
        return 0

    def finish_one(j, total):
        copy(j).wait()
        return total + land_ref[j]

    lax.fori_loop(1, half + 1, start, 0)

    rows = both_ref.shape[1]
    n_mult = (rows - 10) // 7
    n_bond = 2 * width
    n_term = n_mult * n_bond
    total_terms = 2 * n_bond + 7 * n_term
    index = jnp.concatenate(
        [both_ref[k, row : row + 1, :] for row in range(8, rows) for k in range(2)], axis=1
    ).astype(jnp.int32)
    hi_part = index // LANES
    lo_part = index - hi_part * LANES
    lo_rows = lax.broadcasted_iota(jnp.int32, (LANES, total_terms), 0)
    lo_ref[...] = jnp.where(lo_rows == lo_part, 1.0, 0.0).astype(jnp.bfloat16)
    hi_rows = lax.broadcasted_iota(jnp.int32, (high, total_terms), 0)
    hi_ref[...] = jnp.where(hi_rows == hi_part, 1.0, 0.0)
    rest = jnp.concatenate([both_ref[k, 7:8, :] for k in range(2)], axis=1)
    fill = [jnp.zeros((high - used, LANES), jnp.float32)] if high > used else []

    def tiled(read, wanted):
        pieces = []
        for row in wanted:
            for k in range(2):
                for c in range(chunks):
                    pieces.append(read(k, row, c * LANES))
            pieces += fill
        return jnp.concatenate(pieces, axis=0)

    def from_pack(k, row, at):
        return both_ref[k, row : row + 1, at : at + LANES]

    def from_force(k, row, at):
        return force_ref[k, row : row + 1, at : at + LANES]

    mass = tiled(from_pack, (6, 6, 6))

    def push_at(coords):
        looked = merge3(
            jnp.dot(split3(coords), lo_ref[...], preferred_element_type=jnp.float32)
        )
        hi = hi_ref[...]
        row = [
            jnp.sum(looked[c * high : (c + 1) * high] * hi, axis=0, keepdims=True)
            for c in range(3)
        ]
        cuts = [(0, n_bond), (n_bond, 2 * n_bond)]
        cuts += [(2 * n_bond + j * n_term, 2 * n_bond + (j + 1) * n_term) for j in range(7)]
        atoms = [[row[c][:, lo:up] for c in range(3)] for lo, up in cuts]
        pushes = (
            bond_push(atoms[0], atoms[1], rest)
            + angle_push(*atoms[2:5])
            + torsion_push(*atoms[5:9])
        )
        spread = jnp.concatenate(
            [jnp.concatenate([p[c] for p in pushes], axis=1) * hi for c in range(3)], axis=0
        )
        return merge3(
            lax.dot_general(
                split3(spread),
                lo_ref[...],
                (((1,), (1,)), ((), ())),
                preferred_element_type=jnp.float32,
            )
        )

    dt = OUTER_DT / INNER
    x = tiled(from_pack, (0, 1, 2))
    half_step = (0.5 * dt) * mass
    v = tiled(from_pack, (3, 4, 5)) + half_step * push_at(x)

    total = lax.fori_loop(1, half + 1, finish_one, part_ref[:, 0:width])
    force_ref[sub] = total
    swap = pltpu.make_async_remote_copy(
        src_ref=force_ref.at[sub],
        dst_ref=force_ref.at[sub],
        send_sem=force_send,
        recv_sem=force_recv,
        device_id=device_at(place + 1 - 2 * sub),
        device_id_type=MESH,
    )
    swap.start()
    torque = torque_of(
        [total[c : c + 1] for c in range(12)],
        [all_ref[c : c + 1, 0:width] for c in range(4, 7)],
        [all_ref[c : c + 1, 0:width] for c in range(7, 13)],
    )
    swap.wait()
    v = v + (0.5 * OUTER_DT) * tiled(from_force, (0, 1, 2)) * mass

    def substep(step, carry):
        x, v = carry
        x = x + dt * v
        kick = half_step * push_at(x)
        v = v + kick
        v = v + jnp.where(step < INNER - 1, kick, 0.0)
        return x, v

    x, v = lax.fori_loop(0, INNER, substep, (x, v))

    def mine(state):
        rows = []
        for c in range(3):
            sides = [
                jnp.concatenate(
                    [
                        state[c * high + k * chunks + h : c * high + k * chunks + h + 1]
                        for h in range(chunks)
                    ],
                    axis=1,
                )
                for k in range(2)
            ]
            rows.append(jnp.where(sub == 0, sides[0], sides[1]))
        return jnp.concatenate(rows, axis=0)

    out_ref[...] = jnp.concatenate([mine(x), mine(v), total[0:3], torque], axis=0)


def body(
    positions,
    velocities,
    charges,
    dipoles,
    quadrupoles,
    damping,
    inverse_mass,
    bonds,
    bond_length,
    angles,
    torsions,
):
    atoms = positions.shape[1]
    n_sub = lax.axis_size("sub")
    count = lax.axis_size("blk") * lax.axis_size("rep") * n_sub
    slots = count // 2 + 1
    vmem = pl.BlockSpec(memory_space=pltpu.VMEM)
    dma = pltpu.SemaphoreType.DMA
    hbm = pl.BlockSpec(memory_space=pltpu.HBM)
    scalars = jnp.stack([charges, damping, inverse_mass, bond_length])
    index_rows = 2 + (angles.size + torsions.size) // atoms
    pack_rows = 8 + index_rows

    def params(**more):
        return pltpu.CompilerParams(vmem_limit_bytes=48 * 1024 * 1024, **more)

    def shape(*dims):
        return jax.ShapeDtypeStruct(dims, jnp.float32)

    everyone, both, own, near = pl.pallas_call(
        functools.partial(gather_kernel, count),
        out_shape=(
            shape(16, slots * atoms),
            shape(2, pack_rows, atoms),
            shape(atoms, LANES),
            shape(atoms, LANES),
        ),
        in_specs=[hbm] * 4 + [vmem] + [hbm] * 3,
        out_specs=(vmem,) * 4,
        scratch_shapes=[
            pltpu.VMEM(x.shape, x.dtype)
            for x in (positions, velocities, dipoles, quadrupoles, bonds, angles, torsions)
        ]
        + [
            pltpu.VMEM((16, atoms), jnp.float32),
            pltpu.VMEM((pack_rows, atoms), jnp.float32),
            dma((7,)),
            dma((slots,)),
            dma((slots,)),
            dma,
            dma,
        ],
        compiler_params=params(collective_id=1),
        name="gather",
    )(positions, velocities, dipoles, quadrupoles, scalars, bonds, angles, torsions)
    parts = pl.pallas_call(
        functools.partial(pair_kernel, count),
        out_shape=shape(16, slots * atoms),
        in_specs=[vmem] * 3,
        out_specs=vmem,
        scratch_shapes=[
            pltpu.VMEM((96, slots * atoms), jnp.float32),
            pltpu.VMEM((atoms, LANES), jnp.float32),
        ],
        compiler_params=params(),
        name="pairs",
    )(own, near, everyone)
    high = -(-(n_sub * atoms // LANES) // 8) * 8
    total = n_sub * index_rows * atoms
    out = pl.pallas_call(
        functools.partial(final_kernel, count, high),
        out_shape=shape(12, atoms),
        in_specs=[vmem] * 3,
        out_specs=vmem,
        scratch_shapes=[
            pltpu.VMEM((slots, 16, atoms), jnp.float32),
            pltpu.VMEM((2, 16, atoms), jnp.float32),
            pltpu.VMEM((LANES, total), jnp.bfloat16),
            pltpu.VMEM((high, total), jnp.float32),
            dma((slots,)),
            dma((slots,)),
            dma,
            dma,
        ],
        compiler_params=params(collective_id=2),
        name="finale",
    )(parts, both, everyone)
    return tuple(out[3 * n : 3 * n + 3] for n in range(4))


def solution(mesh):
    placed = (
        P(None, ("groups", "blk", "rep", "sub")),
        P(None, ("groups", "blk", "rep", "sub")),
        P(("groups", "blk", "rep", "sub")),
        P(None, ("groups", "blk", "rep", "sub")),
        P(None, ("groups", "blk", "rep", "sub")),
        P(("groups", "blk", "rep", "sub")),
        P(("groups", "blk", "rep", "sub")),
        P(None, ("groups", "blk", "rep", "sub")),
        P(("groups", "blk", "rep", "sub")),
        P(None, ("groups", "blk", "rep", "sub")),
        P(None, ("groups", "blk", "rep", "sub")),
    )
    return jax.shard_map(
        body,
        mesh=mesh,
        in_specs=placed,
        out_specs=(
            P(None, ("groups", "blk", "rep", "sub")),
            P(None, ("groups", "blk", "rep", "sub")),
            P(None, ("groups", "blk", "rep", "sub")),
            P(None, ("groups", "blk", "rep", "sub")),
        ),
        check_vma=False,
    )
```

```python
import functools

import jax
import jax.numpy as jnp
from jax import lax
from jax.experimental import pallas as pl
from jax.experimental.pallas import tpu as pltpu
from jax.sharding import PartitionSpec as P

INNER = 4
MESH = pl.DeviceIdType.MESH
LANES = 128
QUAD_INDEX = ((0, 1, 2), (1, 3, 4), (2, 4, 5))
BOND_K = 0.3
ANGLE_K = 4.0
ANGLE_REST = -0.33
TORSION_K = 2.0
OUTER_DT = 0.2
UNROLL = 7


def dot3(left, right):
    return left[0] * right[0] + left[1] * right[1] + left[2] * right[2]


def matvec(quad, vec):
    return [dot3([quad[QUAD_INDEX[a][b]] for b in range(3)], vec) for a in range(3)]


def my_place():
    n_rep = lax.axis_size("rep")
    n_sub = lax.axis_size("sub")
    return (lax.axis_index("blk") * n_rep + lax.axis_index("rep")) * n_sub + lax.axis_index("sub")


def device_at(place):
    n_rep = lax.axis_size("rep")
    n_sub = lax.axis_size("sub")
    return (
        lax.axis_index("groups"),
        place // (n_rep * n_sub),
        (place // n_sub) % n_rep,
        place % n_sub,
    )


def greet(half, place, count):
    barrier = pltpu.get_barrier_semaphore()

    def one(j, _):
        for other in ((place + j) % count, (place + count - j) % count):
            pl.semaphore_signal(
                barrier, inc=1, device_id=device_at(other), device_id_type=MESH
            )
        return 0

    lax.fori_loop(1, half + 1, one, 0)


def all_here(half):
    pl.semaphore_wait(pltpu.get_barrier_semaphore(), 2 * half)


def gather_kernel(
    count,
    pos_any,
    vel_any,
    dip_any,
    quad_any,
    scal_ref,
    bond_any,
    angle_any,
    torsion_any,
    out_ref,
    both_ref,
    own_ref,
    near_ref,
    pos_ref,
    vel_ref,
    dip_ref,
    quad_ref,
    bond_ref,
    angle_ref,
    torsion_ref,
    record_ref,
    pack_ref,
    local_sem,
    send_sem,
    recv_sem,
    pack_send,
    pack_recv,
):
    half = count // 2
    width = pos_any.shape[1]
    place = my_place()
    sub = lax.axis_index("sub")
    loads = [
        pltpu.make_async_copy(src, dst, local_sem.at[n])
        for n, (src, dst) in enumerate(
            (
                (pos_any, pos_ref),
                (vel_any, vel_ref),
                (dip_any, dip_ref),
                (quad_any, quad_ref),
                (bond_any, bond_ref),
                (angle_any, angle_ref),
                (torsion_any, torsion_ref),
            )
        )
    ]
    for load in loads:
        load.start()
    greet(half, place, count)
    for load in loads:
        load.wait()

    record_ref[...] = jnp.concatenate(
        [
            pos_ref[...],
            scal_ref[0:1, :],
            dip_ref[...],
            quad_ref[...],
            scal_ref[1:2, :],
            jnp.zeros((2, width), jnp.float32),
        ],
        axis=0,
    )

    def copy(j):
        return pltpu.make_async_remote_copy(
            src_ref=record_ref,
            dst_ref=out_ref.at[:, pl.ds(pl.multiple_of(j * width, LANES), width)],
            send_sem=send_sem.at[j],
            recv_sem=recv_sem.at[j],
            device_id=device_at((place + count - j) % count),
            device_id_type=MESH,
        )

    def start(j, _):
        copy(j).start()
        return 0

    def finish_one(j, _):
        copy(j).wait()
        return 0

    def cut(ref):
        whole = ref[...].astype(jnp.float32)
        return [
            whole[row : row + 1, at : at + width]
            for row in range(whole.shape[0])
            for at in range(0, whole.shape[1], width)
        ]

    pack_ref[...] = jnp.concatenate(
        [pos_ref[...], vel_ref[...], scal_ref[2:4, :]]
        + cut(bond_ref)
        + cut(angle_ref)
        + cut(torsion_ref),
        axis=0,
    )
    out_ref[:, 0:width] = record_ref[...]
    both_ref[sub] = pack_ref[...]
    wide = jnp.concatenate([record_ref[...], jnp.zeros((LANES - 16, width), jnp.float32)], axis=0)
    chunks = width // LANES
    for c in range(chunks):
        own_ref[c * LANES : (c + 1) * LANES, :] = wide[:, c * LANES : (c + 1) * LANES].T
    lane = lax.broadcasted_iota(jnp.int32, (8, LANES), 1)
    sublane = lax.broadcasted_iota(jnp.int32, (8, LANES), 0)
    diff = lane - sublane

    def one_group(group, _):
        base = pl.multiple_of(group * 8, 8)
        target = [
            jnp.broadcast_to(own_ref[pl.ds(base, 8), c : c + 1], (8, LANES)) for c in range(14)
        ]

        def near(chunk, sums):
            at = pl.multiple_of(chunk * LANES, LANES)
            source = [record_ref[c : c + 1, pl.ds(at, LANES)] for c in range(14)]

            def alive(root):
                return jnp.where(diff == base - at, 0.0, root)

            push, on_i, _ = pair_terms(target, source, alive)
            return tuple(x + y for x, y in zip(sums, push + on_i))

        sums = lax.fori_loop(0, chunks, near, (jnp.zeros((8, LANES), jnp.float32),) * 12, unroll=True)
        near_ref[pl.ds(base, 8), :] = row_sums(sums)
        return 0

    groups = width // 8
    early = groups // 3
    lax.fori_loop(0, early, one_group, 0)
    all_here(half)
    lax.fori_loop(1, half + 1, start, 0)
    swap = pltpu.make_async_remote_copy(
        src_ref=pack_ref,
        dst_ref=both_ref.at[sub],
        send_sem=pack_send,
        recv_sem=pack_recv,
        device_id=device_at(place + 1 - 2 * sub),
        device_id_type=MESH,
    )
    swap.start()
    lax.fori_loop(early, groups, one_group, 0)
    swap.wait()
    lax.fori_loop(1, half + 1, finish_one, 0)


def row_sums(sums):
    return jnp.concatenate(
        [jnp.sum(x, axis=1, keepdims=True) for x in sums]
        + [jnp.zeros((8, LANES - len(sums)), jnp.float32)],
        axis=1,
    )


def pair_terms(target, source, alive):
    c_i, d_i, q_i = target[3], target[4:7], target[7:13]
    c_k, d_k, q_k = source[3], source[4:7], source[7:13]
    r = [source[c] - target[c] for c in range(3)]
    s = dot3(r, r) + target[13] * source[13]
    root = lax.rsqrt(s)
    b1 = alive(root)
    inv = root * root
    b3 = b1 * inv
    b5 = b3 * (3.0 * inv)
    b7 = b5 * (5.0 * inv)
    b9 = b7 * (7.0 * inv)
    b11 = b9 * (9.0 * inv)
    f5 = 2.0 * b5
    f7 = 4.0 * b7
    f10 = 4.0 * b5
    w = matvec(q_k, r)
    u = matvec(q_i, r)
    dk = dot3(d_k, r)
    qk = dot3(w, r)
    di = dot3(d_i, r)
    qi = dot3(u, r)
    a_i = c_k * b3 - dk * b5 + qk * b7
    b_i = c_k * b5 - dk * b7 + qk * b9
    g_i = c_k * b7 - dk * b9 + qk * b11
    a_k = c_i * b3 + di * b5 + qi * b7
    b_k = c_i * b5 + di * b7 + qi * b9
    h_i = [f5 * d_k[a] - f7 * w[a] for a in range(3)]
    h_k = [f5 * d_i[a] + f7 * u[a] for a in range(3)]
    br_i = [b_i * r[a] for a in range(3)]
    br_k = [b_k * r[a] for a in range(3)]
    v_i = [br_i[a] + h_i[a] for a in range(3)]
    v_k = [br_k[a] - h_k[a] for a in range(3)]
    on_i = matvec(q_i, [v_i[a] + br_i[a] for a in range(3)])
    on_k = matvec(q_k, [v_k[a] + br_k[a] for a in range(3)])
    qm = (q_i[0] * q_k[0] + q_i[3] * q_k[3] + q_i[5] * q_k[5]) + 2.0 * (
        q_i[1] * q_k[1] + q_i[2] * q_k[2] + q_i[4] * q_k[4]
    )
    alpha = (
        c_i * a_i
        + di * b_i
        + qi * g_i
        + 0.5 * (dot3(d_i, h_i) + f7 * (dot3(d_k, u) + qm))
        - (4.0 * b9) * dot3(u, w)
    )
    push = [
        (a_i * d_i[a] - a_k * d_k[a]) + (on_i[a] + on_k[a]) - alpha * r[a] for a in range(3)
    ]

    def quad_rows(v, q):
        return [
            r[0] * v[0] + f5 * q[0],
            (r[0] * v[1] + r[1] * v[0]) + f10 * q[1],
            (r[0] * v[2] + r[2] * v[0]) + f10 * q[2],
            r[1] * v[1] + f5 * q[3],
            (r[1] * v[2] + r[2] * v[1]) + f10 * q[4],
            r[2] * v[2] + f5 * q[5],
        ]

    f_i = [a_i * r[a] + b3 * d_k[a] - f5 * w[a] for a in range(3)]
    f_k = [b3 * d_i[a] + f5 * u[a] - a_k * r[a] for a in range(3)]
    return push, f_i + quad_rows(v_i, q_k), f_k + quad_rows(v_k, q_i)


def pair_kernel(count, own_ref, near_ref, all_ref, out_ref, acc_ref, tgt_ref):
    half = count // 2
    rows = own_ref.shape[0]
    chunks = rows // LANES
    lower = my_place() < half
    acc_ref[...] = jnp.zeros_like(acc_ref)
    zero = jnp.zeros((8, LANES), jnp.float32)

    def source_at(start):
        return [all_ref[c : c + 1, pl.ds(start, LANES)] for c in range(14)]

    def one_group(group, _):
        base = pl.multiple_of(group * 8, 8)
        target = [
            jnp.broadcast_to(own_ref[pl.ds(base, 8), c : c + 1], (8, LANES)) for c in range(14)
        ]

        def far(chunk, sums):
            start = pl.multiple_of(chunk * LANES, LANES)
            push, on_i, on_k = pair_terms(target, source_at(start), lambda root: root)
            for c in range(3):
                acc_ref[8 * c : 8 * c + 8, pl.ds(start, LANES)] -= push[c]
            for c in range(9):
                acc_ref[24 + 8 * c : 32 + 8 * c, pl.ds(start, LANES)] += on_k[c]
            return tuple(x + y for x, y in zip(sums, push + on_i))

        first = lax.rem(base // LANES + jnp.where(lower, 0, 1), 2)

        def last(step, sums):
            return far(half * chunks + first + 2 * step, sums)

        sums = lax.fori_loop(chunks, half * chunks, far, (zero,) * 12, unroll=UNROLL)
        sums = lax.fori_loop(0, (chunks - first + 1) // 2, last, sums)
        tgt_ref[pl.ds(base, 8), :] = near_ref[pl.ds(base, 8), :] + row_sums(sums)
        return 0

    lax.fori_loop(0, rows // 8, one_group, 0)

    def fold(chunk, _):
        at = pl.ds(pl.multiple_of(chunk * LANES, LANES), LANES)
        out_ref[:, at] = jnp.concatenate(
            [jnp.sum(acc_ref[8 * c : 8 * c + 8, at], axis=0, keepdims=True) for c in range(12)]
            + [jnp.zeros((4, LANES), jnp.float32)],
            axis=0,
        )
        return 0

    lax.fori_loop(chunks, (half + 1) * chunks, fold, 0)
    for c in range(chunks):
        flipped = tgt_ref[c * LANES : (c + 1) * LANES, :].T
        out_ref[:, c * LANES : (c + 1) * LANES] = flipped[0:16]


def torque_of(sums, d, q):
    field = [-sums[3 + a] for a in range(3)]
    halves = (1.0, 0.5, 0.5, 1.0, 0.5, 1.0)
    g = [halves[c] * sums[6 + c] for c in range(6)]

    def product(a, b):
        return dot3(
            [q[QUAD_INDEX[a][c]] for c in range(3)], [g[QUAD_INDEX[c][b]] for c in range(3)]
        )

    return jnp.concatenate(
        [
            d[1] * field[2] - d[2] * field[1] - 2.0 * (product(1, 2) - product(2, 1)),
            d[2] * field[0] - d[0] * field[2] - 2.0 * (product(2, 0) - product(0, 2)),
            d[0] * field[1] - d[1] * field[0] - 2.0 * (product(0, 1) - product(1, 0)),
        ],
        axis=0,
    )


def cross3(a, b):
    return [
        a[1] * b[2] - a[2] * b[1],
        a[2] * b[0] - a[0] * b[2],
        a[0] * b[1] - a[1] * b[0],
    ]


def minus(a, b):
    return [x - y for x, y in zip(a, b)]


def bond_push(first, second, rest):
    step = minus(second, first)
    sq = dot3(step, step) + 0.01
    scale = BOND_K * (1.0 - rest * lax.rsqrt(sq))
    pull = [scale * x for x in step]
    return [pull, [-x for x in pull]]


def angle_push(first, centre, third):
    a = minus(first, centre)
    b = minus(third, centre)
    ia = lax.rsqrt(dot3(a, a) + 0.01)
    ib = lax.rsqrt(dot3(b, b) + 0.01)
    cosine = dot3(a, b) * (ia * ib)
    lead = -ANGLE_K * (cosine - ANGLE_REST)
    both = lead * (ia * ib)
    on_a = lead * cosine * (ia * ia)
    on_b = lead * cosine * (ib * ib)
    fa = [both * y - on_a * x for x, y in zip(a, b)]
    fb = [both * x - on_b * y for x, y in zip(a, b)]
    return [fa, [-x - y for x, y in zip(fa, fb)], fb]


def torsion_push(p0, p1, p2, p3):
    one = minus(p1, p0)
    two = minus(p2, p1)
    three = minus(p3, p2)
    m = cross3(one, two)
    n = cross3(two, three)
    im = lax.rsqrt(dot3(m, m) + 0.1)
    in_ = lax.rsqrt(dot3(n, n) + 0.1)
    both = -TORSION_K * (im * in_)
    dih = dot3(m, n) * both
    cm = dih * (im * im)
    cn = dih * (in_ * in_)
    gm = [both * y - cm * x for x, y in zip(m, n)]
    gn = [both * x - cn * y for x, y in zip(m, n)]
    f_one = cross3(two, gm)
    f_three = cross3(gn, two)
    f_two = [x + y for x, y in zip(cross3(gm, one), cross3(three, gn))]
    return [
        [-x for x in f_one],
        minus(f_one, f_two),
        minus(f_two, f_three),
        f_three,
    ]


def split3(x):
    top = x.astype(jnp.bfloat16)
    rest = x - top.astype(jnp.float32)
    mid = rest.astype(jnp.bfloat16)
    low = (rest - mid.astype(jnp.float32)).astype(jnp.bfloat16)
    return jnp.concatenate([top, mid, low], axis=0)


def merge3(x):
    n = x.shape[0] // 3
    return x[0:n] + x[n : 2 * n] + x[2 * n : 3 * n]


def final_kernel(
    count,
    high,
    part_ref,
    both_ref,
    all_ref,
    out_ref,
    land_ref,
    force_ref,
    lo_ref,
    hi_ref,
    send_sem,
    recv_sem,
    force_send,
    force_recv,
):
    half = count // 2
    width = out_ref.shape[1]
    chunks = width // LANES
    used = 2 * chunks
    place = my_place()
    sub = lax.axis_index("sub")
    greet(half, place, count)

    def copy(j):
        return pltpu.make_async_remote_copy(
            src_ref=part_ref.at[:, pl.ds(pl.multiple_of(j * width, LANES), width)],
            dst_ref=land_ref.at[j],
            send_sem=send_sem.at[j],
            recv_sem=recv_sem.at[j],
            device_id=device_at((place + j) % count),
            device_id_type=MESH,
        )

    def start(j, _):
        copy(j).start()
        return 0

    def finish_one(j, total):
        copy(j).wait()
        return total + land_ref[j]

    rows = both_ref.shape[1]
    n_mult = (rows - 10) // 7
    n_bond = 2 * width
    n_term = n_mult * n_bond
    total_terms = 2 * n_bond + 7 * n_term
    index = jnp.concatenate(
        [both_ref[k, row : row + 1, :] for row in range(8, rows) for k in range(2)], axis=1
    ).astype(jnp.int32)
    hi_part = index // LANES
    lo_part = index - hi_part * LANES
    lo_rows = lax.broadcasted_iota(jnp.int32, (LANES, total_terms), 0)
    lo_ref[...] = jnp.where(lo_rows == lo_part, 1.0, 0.0).astype(jnp.bfloat16)
    hi_rows = lax.broadcasted_iota(jnp.int32, (high, total_terms), 0)
    hi_ref[...] = jnp.where(hi_rows == hi_part, 1.0, 0.0)
    rest = jnp.concatenate([both_ref[k, 7:8, :] for k in range(2)], axis=1)
    fill = [jnp.zeros((high - used, LANES), jnp.float32)] if high > used else []

    def tiled(read, wanted):
        pieces = []
        for row in wanted:
            for k in range(2):
                for c in range(chunks):
                    pieces.append(read(k, row, c * LANES))
            pieces += fill
        return jnp.concatenate(pieces, axis=0)

    def from_pack(k, row, at):
        return both_ref[k, row : row + 1, at : at + LANES]

    def from_force(k, row, at):
        return force_ref[k, row : row + 1, at : at + LANES]

    mass = tiled(from_pack, (6, 6, 6))
    all_here(half)
    lax.fori_loop(1, half + 1, start, 0)

    def push_at(coords):
        looked = merge3(
            jnp.dot(split3(coords), lo_ref[...], preferred_element_type=jnp.float32)
        )
        hi = hi_ref[...]
        row = [
            jnp.sum(looked[c * high : (c + 1) * high] * hi, axis=0, keepdims=True)
            for c in range(3)
        ]
        cuts = [(0, n_bond), (n_bond, 2 * n_bond)]
        cuts += [(2 * n_bond + j * n_term, 2 * n_bond + (j + 1) * n_term) for j in range(7)]
        atoms = [[row[c][:, lo:up] for c in range(3)] for lo, up in cuts]
        pushes = (
            bond_push(atoms[0], atoms[1], rest)
            + angle_push(*atoms[2:5])
            + torsion_push(*atoms[5:9])
        )
        spread = jnp.concatenate(
            [jnp.concatenate([p[c] for p in pushes], axis=1) * hi for c in range(3)], axis=0
        )
        return merge3(
            lax.dot_general(
                split3(spread),
                lo_ref[...],
                (((1,), (1,)), ((), ())),
                preferred_element_type=jnp.float32,
            )
        )

    dt = OUTER_DT / INNER
    x = tiled(from_pack, (0, 1, 2))
    half_step = (0.5 * dt) * mass
    v = tiled(from_pack, (3, 4, 5)) + half_step * push_at(x)

    total = lax.fori_loop(1, half + 1, finish_one, part_ref[:, 0:width])
    force_ref[sub] = total
    swap = pltpu.make_async_remote_copy(
        src_ref=force_ref.at[sub],
        dst_ref=force_ref.at[sub],
        send_sem=force_send,
        recv_sem=force_recv,
        device_id=device_at(place + 1 - 2 * sub),
        device_id_type=MESH,
    )
    swap.start()
    torque = torque_of(
        [total[c : c + 1] for c in range(12)],
        [all_ref[c : c + 1, 0:width] for c in range(4, 7)],
        [all_ref[c : c + 1, 0:width] for c in range(7, 13)],
    )
    swap.wait()
    v = v + (0.5 * OUTER_DT) * tiled(from_force, (0, 1, 2)) * mass

    def substep(step, carry):
        x, v = carry
        x = x + dt * v
        kick = half_step * push_at(x)
        v = v + kick
        v = v + jnp.where(step < INNER - 1, kick, 0.0)
        return x, v

    x, v = lax.fori_loop(0, INNER, substep, (x, v))

    def mine(state):
        rows = []
        for c in range(3):
            sides = [
                jnp.concatenate(
                    [
                        state[c * high + k * chunks + h : c * high + k * chunks + h + 1]
                        for h in range(chunks)
                    ],
                    axis=1,
                )
                for k in range(2)
            ]
            rows.append(jnp.where(sub == 0, sides[0], sides[1]))
        return jnp.concatenate(rows, axis=0)

    out_ref[...] = jnp.concatenate([mine(x), mine(v), total[0:3], torque], axis=0)


def body(
    positions,
    velocities,
    charges,
    dipoles,
    quadrupoles,
    damping,
    inverse_mass,
    bonds,
    bond_length,
    angles,
    torsions,
):
    atoms = positions.shape[1]
    n_sub = lax.axis_size("sub")
    count = lax.axis_size("blk") * lax.axis_size("rep") * n_sub
    slots = count // 2 + 1
    vmem = pl.BlockSpec(memory_space=pltpu.VMEM)
    dma = pltpu.SemaphoreType.DMA
    hbm = pl.BlockSpec(memory_space=pltpu.HBM)
    scalars = jnp.stack([charges, damping, inverse_mass, bond_length])
    index_rows = 2 + (angles.size + torsions.size) // atoms
    pack_rows = 8 + index_rows

    def params(**more):
        return pltpu.CompilerParams(vmem_limit_bytes=48 * 1024 * 1024, **more)

    def shape(*dims):
        return jax.ShapeDtypeStruct(dims, jnp.float32)

    everyone, both, own, near = pl.pallas_call(
        functools.partial(gather_kernel, count),
        out_shape=(
            shape(16, slots * atoms),
            shape(2, pack_rows, atoms),
            shape(atoms, LANES),
            shape(atoms, LANES),
        ),
        in_specs=[hbm] * 4 + [vmem] + [hbm] * 3,
        out_specs=(vmem,) * 4,
        scratch_shapes=[
            pltpu.VMEM(x.shape, x.dtype)
            for x in (positions, velocities, dipoles, quadrupoles, bonds, angles, torsions)
        ]
        + [
            pltpu.VMEM((16, atoms), jnp.float32),
            pltpu.VMEM((pack_rows, atoms), jnp.float32),
            dma((7,)),
            dma((slots,)),
            dma((slots,)),
            dma,
            dma,
        ],
        compiler_params=params(collective_id=1),
        name="gather",
    )(positions, velocities, dipoles, quadrupoles, scalars, bonds, angles, torsions)
    parts = pl.pallas_call(
        functools.partial(pair_kernel, count),
        out_shape=shape(16, slots * atoms),
        in_specs=[vmem] * 3,
        out_specs=vmem,
        scratch_shapes=[
            pltpu.VMEM((96, slots * atoms), jnp.float32),
            pltpu.VMEM((atoms, LANES), jnp.float32),
        ],
        compiler_params=params(),
        name="pairs",
    )(own, near, everyone)
    high = -(-(n_sub * atoms // LANES) // 8) * 8
    total = n_sub * index_rows * atoms
    out = pl.pallas_call(
        functools.partial(final_kernel, count, high),
        out_shape=shape(12, atoms),
        in_specs=[vmem] * 3,
        out_specs=vmem,
        scratch_shapes=[
            pltpu.VMEM((slots, 16, atoms), jnp.float32),
            pltpu.VMEM((2, 16, atoms), jnp.float32),
            pltpu.VMEM((LANES, total), jnp.bfloat16),
            pltpu.VMEM((high, total), jnp.float32),
            dma((slots,)),
            dma((slots,)),
            dma,
            dma,
        ],
        compiler_params=params(collective_id=2),
        name="finale",
    )(parts, both, everyone)
    return tuple(out[3 * n : 3 * n + 3] for n in range(4))


def solution(mesh):
    placed = (
        P(None, ("groups", "blk", "rep", "sub")),
        P(None, ("groups", "blk", "rep", "sub")),
        P(("groups", "blk", "rep", "sub")),
        P(None, ("groups", "blk", "rep", "sub")),
        P(None, ("groups", "blk", "rep", "sub")),
        P(("groups", "blk", "rep", "sub")),
        P(("groups", "blk", "rep", "sub")),
        P(None, ("groups", "blk", "rep", "sub")),
        P(("groups", "blk", "rep", "sub")),
        P(None, ("groups", "blk", "rep", "sub")),
        P(None, ("groups", "blk", "rep", "sub")),
    )
    return jax.shard_map(
        body,
        mesh=mesh,
        in_specs=placed,
        out_specs=(
            P(None, ("groups", "blk", "rep", "sub")),
            P(None, ("groups", "blk", "rep", "sub")),
            P(None, ("groups", "blk", "rep", "sub")),
            P(None, ("groups", "blk", "rep", "sub")),
        ),
        check_vma=False,
    )
```
